32 devices in a mesh: row: 8 (over y, x, core), col: 4 (over z).
Axes of the slice: x: 2, y: 2, z: 4, core: 2. Of those that a mesh axis runs over, the one named last changes fastest.
Arguments:
- pair: bfloat16 [64, 64, 128], P('row', 'col'), may hold values from -6 to 6
- pair_mask: int32 [64, 64], P('row', 'col'), may hold values 0 or 1
- ln_in_gain: float32 [128], replicated, may hold values from 0.1 to 1.9
- ln_in_bias: float32 [128], replicated, may hold values from -3 to 3
- w_proj: bfloat16 [128, 512], replicated, may hold values from -0.5 to 0.5
- b_proj: float32 [512], replicated, may hold values from -3 to 3
- w_gate: bfloat16 [128, 128], replicated, may hold values from -0.5 to 0.5
- b_gate: float32 [128], replicated, may hold values from -3 to 3
- ln_mid_gain: float32 [128], replicated, may hold values from 0.1 to 1.9
- ln_mid_bias: float32 [128], replicated, may hold values from -3 to 3
- w_out: bfloat16 [128, 128], replicated, may hold values from -0.5 to 0.5
- b_out: float32 [128], replicated, may hold values from -3 to 3
- cotangent: bfloat16 [64, 64, 128], P('row', 'col'), may hold values from -6 to 6
Outputs:
- update: bfloat16 [64, 64, 128], P('row', 'col')
- pair_grad: float32 [64, 64, 128], P('row', 'col')
The draws below stay inside these ranges and needn't reach their ends.
All inputs are finite; a program needn't handle non-finite values. No bound on the sum of `pair_mask` on one device may be relied on, other than what follows from the above.
Results may differ from the reference program's by a relative error of at most 0.019.
Values may be sent and summed in bfloat16 or wider, within the bound.
A program may use at most 64 MiB of HBM per device.

```python
import jax
import jax.numpy as jnp
from jax import lax

C = 128
H = 128
TILE_I = 8
N = 64
N_ROW = 8


def set_ends(entries, key, low, top_value):
    index_at = [jax.random.randint(jax.random.fold_in(key, axis), (), 0, length) for axis, length in enumerate(entries.shape)]
    widest = entries.shape.index(max(entries.shape))
    neighbour = index_at[:widest] + [(index_at[widest] + 1) % entries.shape[widest]] + index_at[widest + 1:]
    return entries.at[tuple(index_at)].set(low).at[tuple(neighbour)].set(top_value)


def block_levels(stream_key, shape, shards, low, top_value):
    def one(position, parts):
        steps = jax.random.uniform(jax.random.fold_in(jax.random.fold_in(stream_key, 6), position), (parts,), jnp.float32, low / len(shards), top_value / len(shards))
        return jnp.repeat(jnp.exp(steps), shape[position] // parts).reshape((-1,) + (1,) * (len(shape) - position - 1))

    level = one(*shards[0])
    for cut in shards[1:]:
        level = level * one(*cut)
    return level


def normal_values(key, shape, spread, reach, pieces=(), dtype=jnp.bfloat16):
    array = jax.random.normal(key, shape, jnp.float32) * spread
    if len(pieces) > 0:
        array = block_levels(key, shape, pieces, -0.22, 0.18) * array
    return jnp.clip(array, min=-reach, max=reach).astype(dtype)


def setup_inputs(seed: int = 0) -> dict:
    seeds = jax.random.split(jax.random.key(seed), 14)
    pair = normal_values(seeds[0], (N, N, C), 1.0, 6.0, ((0, 8), (1, 4)))
    pair_mask = set_ends((jax.random.randint(seeds[1], (N, N), 0, 8) < 7).astype(jnp.int32), jax.random.fold_in(seeds[1], 1), 0, 1)
    ln_in_gain = jnp.clip(1.0 + 0.18 * jax.random.normal(seeds[2], (C,), jnp.float32), 0.1, 1.9)
    ln_in_bias = normal_values(seeds[3], (C,), 0.5, 3.0, (), jnp.float32)
    w_proj = normal_values(seeds[4], (C, 4 * H), C ** -0.5, 0.5)
    b_proj = normal_values(seeds[5], (4 * H,), 0.5, 3.0, (), jnp.float32)
    w_gate = normal_values(seeds[6], (C, C), C ** -0.5, 0.5)
    b_gate = normal_values(seeds[7], (C,), 0.5, 3.0, (), jnp.float32)
    ln_mid_gain = jnp.clip(1.0 + 0.18 * jax.random.normal(seeds[8], (H,), jnp.float32), 0.1, 1.9)
    ln_mid_bias = normal_values(seeds[9], (H,), 0.5, 3.0, (), jnp.float32)
    w_out = normal_values(seeds[10], (H, C), H ** -0.5, 0.5)
    b_out = normal_values(seeds[11], (C,), 0.5, 3.0, (), jnp.float32)
    cotangent = normal_values(seeds[12], (N, N, C), 1.0, 6.0, ((0, 8), (1, 4)))
    return dict(pair=pair, pair_mask=pair_mask, ln_in_gain=ln_in_gain, ln_in_bias=ln_in_bias, w_proj=w_proj, b_proj=b_proj, w_gate=w_gate, b_gate=b_gate, ln_mid_gain=ln_mid_gain, ln_mid_bias=ln_mid_bias, w_out=w_out, b_out=b_out, cotangent=cotangent)


def layer_norm(values, gain_vec, bias_vec):
    average = lax.optimization_barrier(jnp.mean(values, -1, keepdims=True))
    centred = values - average
    inv_std = lax.rsqrt(lax.optimization_barrier(jnp.mean(centred * centred, -1, keepdims=True)) + 1e-05)
    hat_val = centred * inv_std
    return (hat_val * gain_vec + bias_vec, hat_val, inv_std)

def norm_back(upstream, hat_val, inv_std, gain_vec):
    scaled = upstream * gain_vec
    return inv_std * (scaled - lax.optimization_barrier(jnp.mean(scaled, -1, keepdims=True)) - hat_val * lax.optimization_barrier(jnp.mean(scaled * hat_val, -1, keepdims=True)))

def gate_pair(proj, mask_f):
    hidden = proj.shape[-1] // 4
    sig_a = jax.nn.sigmoid(proj[..., :hidden])
    sig_b = jax.nn.sigmoid(proj[..., 2 * hidden:3 * hidden])
    a_bf = (mask_f * sig_a * proj[..., hidden:2 * hidden]).astype(jnp.bfloat16)
    b_bf = (mask_f * sig_b * proj[..., 3 * hidden:]).astype(jnp.bfloat16)
    return (a_bf, b_bf)

def gate_back(grad_a, grad_b, proj, mask_f):
    hidden = proj.shape[-1] // 4
    sig_a = jax.nn.sigmoid(proj[..., :hidden])
    val_a = proj[..., hidden:2 * hidden]
    sig_b = jax.nn.sigmoid(proj[..., 2 * hidden:3 * hidden])
    val_b = proj[..., 3 * hidden:]
    masked_a = grad_a * mask_f
    masked_b = grad_b * mask_f
    return jnp.concatenate([masked_a * val_a * sig_a * (1.0 - sig_a), masked_a * sig_a, masked_b * val_b * sig_b * (1.0 - sig_b), masked_b * sig_b], -1)

def reference(pair, pair_mask, ln_in_gain, ln_in_bias, w_proj, b_proj, w_gate, b_gate, ln_mid_gain, ln_mid_bias, w_out, b_out, cotangent):
    normed, hat_in, rstd_in = layer_norm(pair.astype(jnp.float32), ln_in_gain, ln_in_bias)
    x_bf = normed.astype(jnp.bfloat16)
    proj = jnp.dot(x_bf, w_proj, preferred_element_type=jnp.float32) + b_proj
    mask_f = pair_mask.astype(jnp.float32)[..., None]
    a_bf, b_bf = gate_pair(proj, mask_f)
    triangle = jnp.einsum('ikh,jkh->ijh', a_bf.astype(jnp.float32), b_bf.astype(jnp.float32))
    mid_val, hat_mid, rstd_mid = layer_norm(triangle, ln_mid_gain, ln_mid_bias)
    mid_bf = mid_val.astype(jnp.bfloat16)
    out_lin = jnp.dot(mid_bf, w_out, preferred_element_type=jnp.float32) + b_out
    gate = jax.nn.sigmoid(jnp.dot(x_bf, w_gate, preferred_element_type=jnp.float32) + b_gate)
    update = (gate * out_lin).astype(jnp.bfloat16)
    grad_out = cotangent.astype(jnp.float32)
    d_out = (grad_out * gate).astype(jnp.bfloat16)
    d_gpre = (grad_out * out_lin * gate * (1.0 - gate)).astype(jnp.bfloat16)
    d_mid = jnp.dot(d_out, w_out.T, preferred_element_type=jnp.float32)
    d_tri = norm_back(d_mid, hat_mid, rstd_mid, ln_mid_gain).astype(jnp.bfloat16)
    grad_a = jnp.einsum('ijh,jkh->ikh', d_tri.astype(jnp.float32), b_bf.astype(jnp.float32))
    total = N
    hidden = a_bf.shape[-1]
    tri_blocks = d_tri.reshape(N_ROW, TILE_I, total, hidden)
    a_blocks = a_bf.reshape(N_ROW, TILE_I, total, hidden)

    def add_block(running, blocks):
        tri_part, a_part = blocks
        partial_value = jnp.einsum('ijh,ikh->jkh', tri_part.astype(jnp.float32), a_part.astype(jnp.float32))
        rounded = lax.optimization_barrier(partial_value.astype(jnp.bfloat16))
        return (running + rounded.astype(jnp.float32), None)
    grad_b, _ = lax.scan(add_block, jnp.zeros((total, total, hidden), jnp.float32), (tri_blocks, a_blocks))
    d_proj = gate_back(grad_a, grad_b, proj, mask_f).astype(jnp.bfloat16)
    d_x = jnp.dot(d_proj, w_proj.T, preferred_element_type=jnp.float32) + jnp.dot(d_gpre, w_gate.T, preferred_element_type=jnp.float32)
    pair_grad = norm_back(d_x, hat_in, rstd_in, ln_in_gain)
    return (update, pair_grad)
```

```python
import functools

import jax
import jax.numpy as jnp
from jax import lax
from jax.experimental import pallas as pl
from jax.experimental.pallas import tpu as pltpu
from jax.sharding import PartitionSpec as P

F32 = jnp.float32
BF16 = jnp.bfloat16
MESH = pl.DeviceIdType.MESH


def flip(index, step, size):
    if size & (size - 1):
        return lax.rem(index + step, size)
    partner, weight = 0, 1
    while weight < size:
        mine, other = (index // weight) % 2, (step // weight) % 2
        partner = partner + weight * ((mine + other) % 2)
        weight *= 2
    return partner


def source(index, step, size):
    if size & (size - 1):
        return lax.rem(index + size - step, size)
    return flip(index, step, size)


def normalize(values):
    centred = values - jnp.mean(values, -1, keepdims=True)
    inv_std = lax.rsqrt(jnp.mean(centred * centred, -1, keepdims=True) + 1e-05)
    return centred * inv_std, inv_std


def norm_back(upstream, hat, inv_std, gain):
    scaled = upstream * gain
    return inv_std * (
        scaled
        - jnp.mean(scaled, -1, keepdims=True)
        - hat * jnp.mean(scaled * hat, -1, keepdims=True)
    )


def dot(lhs, rhs):
    return jnp.dot(lhs, rhs, preferred_element_type=F32)


def dot_t(lhs, rhs):
    return lax.dot_general(lhs, rhs, (((1,), (1,)), ((), ())), preferred_element_type=F32)


def kernel(
    n_row, n_col, ti, tj,
    pair_hbm, mask_hbm, gin_hbm, bin_hbm, wp_hbm, bp_hbm, wg_hbm, bg_hbm,
    gmid_hbm, bmid_hbm, wo_hbm, bo_hbm, cot_hbm,
    upd_ref, grad_ref,
    pair_ref, mask_ref, gin_ref, bin_ref, wp_ref, bp_ref, wg_ref, bg_ref,
    gmid_ref, bmid_ref, wo_ref, bo_ref, cot_ref, in_sem,
    stage, a_out, a_in, a_f, b_out, b_in, b_f, tri_own, tri_out, tri_in,
    go_out, go_in, dm_f, d_out_s, dz_in, dn_in, d_f, ol_f, ol_out, ol_all, da_f, da_out, da_in,
    a_ss, a_rs, af_ss, b_ss, b_rs, t_ss, t_rs, z_ss, z_rs, n_ss, n_rs, c_ss, c_rs,
):
    row, col = lax.axis_index("row"), lax.axis_index("col")
    chip, core = row // 2, row % 2
    partner = row + 1 - 2 * core
    tok = ti * tj
    half = ti * ti
    chips = n_row // 2
    hid = a_out.shape[-1]

    operands = (
        (pair_hbm, pair_ref), (wp_hbm, wp_ref), (gin_hbm, gin_ref), (bin_hbm, bin_ref),
        (bp_hbm, bp_ref), (mask_hbm, mask_ref), (wg_hbm, wg_ref), (bg_hbm, bg_ref),
        (cot_hbm, cot_ref), (wo_hbm, wo_ref), (gmid_hbm, gmid_ref), (bmid_hbm, bmid_ref),
        (bo_hbm, bo_ref),
    )
    loads = [
        pltpu.make_async_copy(src, dst, in_sem.at[n]) for n, (src, dst) in enumerate(operands)
    ]
    for load in loads:
        load.start()

    barrier = pltpu.get_barrier_semaphore()
    pl.semaphore_signal(barrier, inc=1, device_id=(partner, col), device_id_type=MESH)
    for step in range(1, chips):
        to = 2 * flip(chip, step, chips) + core
        pl.semaphore_signal(barrier, inc=1, device_id=(to, col), device_id_type=MESH)
    for step in range(1, n_col):
        pl.semaphore_signal(barrier, inc=1, device_id=(row, flip(col, step, n_col)), device_id_type=MESH)

    def remote(src, dst, send, recv, to_row, to_col):
        return pltpu.make_async_remote_copy(
            src, dst, send, recv, device_id=(to_row, to_col), device_id_type=MESH
        )

    def reorder(ref):
        stage[...] = ref[...].astype(F32).reshape(tok, hid)
        return jnp.concatenate([stage[pl.ds(k, ti, stride=tj), :] for k in range(tj)], 0)

    loads[0].wait()
    hat_in, rstd_in = normalize(reorder(pair_ref))
    for load in loads[1:6]:
        load.wait()
    x_bf = (hat_in * gin_ref[...] + bin_ref[...]).astype(BF16)
    proj_b = dot(x_bf, wp_ref[:, 2 * hid :]) + bp_ref[:, 2 * hid :]
    mask_v = mask_ref[...].astype(F32)
    mask = jnp.concatenate(
        [jnp.broadcast_to(mask_v[:, k : k + 1], (ti, hid)) for k in range(tj)], 0
    )
    sig_b = jax.nn.sigmoid(proj_b[:, :hid])
    val_b = proj_b[:, hid:]
    b_bf = (mask * sig_b * val_b).astype(BF16)
    b_out[...] = b_bf

    pl.semaphore_wait(barrier, chips + n_col - 1)

    def send_b(step):
        to = flip(chip, step, chips)
        return remote(b_out, b_in.at[chip], b_ss.at[step], b_rs.at[chip], 2 * to + core, col)

    for step in range(1, chips):
        send_b(step).start()

    proj_a = dot(x_bf, wp_ref[:, : 2 * hid]) + bp_ref[:, : 2 * hid]
    sig_a = jax.nn.sigmoid(proj_a[:, :hid])
    val_a = proj_a[:, hid:]
    a_bf = (mask * sig_a * val_a).astype(BF16)
    a_out[...] = a_bf

    def send_a(step):
        to = 2 * flip(chip, step, chips) + core if step else partner
        return remote(a_out, a_in.at[chip, core], a_ss.at[step], a_rs.at[chip, core], to, col)

    def relay_a(step):
        source_chip = source(chip, step, chips)
        held = a_in.at[source_chip, core]
        return remote(held, held, af_ss.at[source_chip], a_rs.at[source_chip, core], partner, col)

    def got_a(source_chip, source_core):
        return remote(
            a_out, a_in.at[source_chip, source_core], a_ss.at[0],
            a_rs.at[source_chip, source_core], partner, col,
        )

    for step in range(chips):
        send_a(step).start()
    a_f[chip, :, core] = a_bf.astype(F32).reshape(tj, ti, hid)
    b_f[chip] = b_bf.astype(F32)

    for load in loads[6:]:
        load.wait()
    gate = jax.nn.sigmoid(dot(x_bf, wg_ref[...]) + bg_ref[...])
    grad_out = reorder(cot_ref)
    go_out[...] = (grad_out * gate).astype(BF16).reshape(2, half, hid)
    send_go = remote(go_out.at[1 - core], go_in, c_ss.at[0], c_rs.at[0], partner, col)
    send_go.start()
    dm_f[:, core] = dot_t(go_out[core], wo_ref[...]).reshape(ti, ti, hid)

    def send_tri(block):
        return remote(
            tri_out.at[block], tri_in.at[col], t_ss.at[block], t_rs.at[col], row, block
        )

    def forward(block):
        sums = []
        a_k = [[a_f[chip, k, part] for part in range(2)] for k in range(tj)]
        for jj in range(ti):
            total = [None, None]
            for k in range(tj):
                b_row = b_f[block, k * ti + jj : k * ti + jj + 1, :]
                for part in range(2):
                    term = a_k[k][part] * b_row
                    total[part] = term if k == 0 else total[part] + term
            sums += total
        whole = jnp.concatenate(sums, 0)

        @pl.when(block == col)
        def _():
            tri_own[...] = whole

        @pl.when(block != col)
        def _():
            tri_out[block] = whole.astype(BF16)
            send_tri(block).start()

    got_a(chip, 1 - core).wait_recv()
    a_f[chip, :, 1 - core] = a_in[chip, 1 - core].astype(F32).reshape(tj, ti, hid)
    forward(chip)

    def forward_step(step, carry):
        block = source(chip, step, chips)
        remote(
            b_out, b_in.at[block], b_ss.at[step], b_rs.at[block], 2 * block + core, col
        ).wait_recv()
        b_f[block] = b_in[block].astype(F32)
        forward(block)
        return carry

    lax.fori_loop(1, chips, forward_step, 0)

    send_go.wait_recv()
    dm_f[:, 1 - core] = dot_t(go_in[...], wo_ref[...]).reshape(ti, ti, hid)
    scaled = dm_f[...].reshape(tok, hid) * gmid_ref[...]
    scaled = scaled - jnp.mean(scaled, -1, keepdims=True)

    for step in range(1, chips):
        source_chip = source(chip, step, chips)
        got_a(source_chip, core).wait_recv()
        relay_a(step).start()
        a_f[source_chip, :, core] = a_in[source_chip, core].astype(F32).reshape(tj, ti, hid)

    triangle = tri_own[...]
    for step in range(1, n_col):
        other = source(col, step, n_col)
        remote(
            tri_out.at[0], tri_in.at[other], t_ss.at[0], t_rs.at[other], row, other
        ).wait_recv()
        triangle = triangle + tri_in[other].astype(F32)
    centred = triangle - jnp.mean(triangle, -1, keepdims=True)
    variance = jnp.mean(centred * centred, -1, keepdims=True)
    slope = jnp.mean(scaled * centred, -1, keepdims=True)
    rstd_mid = lax.rsqrt(variance + 1e-05)
    hat_mid = centred * rstd_mid
    d_tri = (rstd_mid * (scaled - hat_mid * (rstd_mid * slope))).astype(BF16)
    d_out_s[...] = d_tri

    def send_z(step):
        to = flip(col, step, n_col)
        return remote(d_out_s, dz_in.at[col], z_ss.at[step], z_rs.at[col], row, to)

    def send_n(block):
        return remote(
            d_out_s, dn_in.at[chip], n_ss.at[block], n_rs.at[chip], 2 * col + core, block
        )

    for step in reversed(range(1, n_col)):
        send_z(step).start()
    for step in reversed(range(n_col)):
        block = flip(col, step, n_col)
        if step == 0:
            @pl.when(chip != col)
            def _():
                send_n(block).start()

            @pl.when(chip == col)
            def _():
                dn_in[chip] = d_tri
        else:
            send_n(block).start()

    mid_bf = (hat_mid * gmid_ref[...] + bmid_ref[...]).astype(BF16)
    ol_f[...] = (dot(mid_bf, wo_ref[...]) + bo_ref[...]).reshape(ti, 2, ti, hid)
    ol_out[...] = ol_f[:, 1 - core].reshape(half, hid)
    send_ol = remote(ol_out, ol_all.at[core], c_ss.at[1], c_rs.at[1], partner, col)
    send_ol.start()
    ol_all[core] = ol_f[:, core].reshape(half, hid)

    def backward_a(block, d_block, sums):
        out = list(sums)
        for jj in range(ti):
            d_j = [d_block[(2 * jj + part) * ti : (2 * jj + part + 1) * ti] for part in range(2)]
            for k in range(tj):
                b_row = b_f[block, k * ti + jj : k * ti + jj + 1, :]
                for part in range(2):
                    out[2 * k + part] = out[2 * k + part] + d_j[part] * b_row
        return tuple(out)

    zero = tuple(jnp.zeros((ti, hid), F32) for _ in range(2 * tj))
    sums_a = backward_a(col, d_tri.astype(F32), zero)

    for step in range(1, chips):
        source_chip = source(chip, step, chips)
        got_a(source_chip, 1 - core).wait_recv()
        a_f[source_chip, :, 1 - core] = a_in[source_chip, 1 - core].astype(F32).reshape(tj, ti, hid)

    send_ol.wait_recv()
    out_lin = ol_all[...].reshape(tok, hid)
    update = gate * out_lin
    for k in range(tj):
        stage[pl.ds(k, ti, stride=tj), :] = update[k * ti : (k + 1) * ti, :]
    upd_ref[...] = stage[...].astype(BF16).reshape(ti, tj, hid)
    d_gpre = (grad_out * out_lin * gate * (1.0 - gate)).astype(BF16)
    d_x = dot_t(d_gpre, wg_ref[...])

    def backward_step(step, sums):
        other = source(col, step, n_col)
        remote(
            d_out_s, dz_in.at[other], z_ss.at[step], z_rs.at[other], row, other
        ).wait_recv()
        return backward_a(other, dz_in[other].astype(F32), sums)

    sums_a = lax.fori_loop(1, n_col, backward_step, sums_a)
    da_f[...] = jnp.concatenate(sums_a, 0).reshape(tj, 2, ti, hid)
    da_out[...] = da_f[:, 1 - core].reshape(tok, hid)
    send_da = remote(da_out, da_in, c_ss.at[2], c_rs.at[2], partner, col)
    send_da.start()

    def backward_b(step, sums):
        block = source(chip, step, chips)

        @pl.when(jnp.logical_or(block != chip, chip != col))
        def _():
            remote(
                d_out_s, dn_in.at[block], n_ss.at[0], n_rs.at[block], 2 * block + core, chip
            ).wait_recv()

        d_f[...] = dn_in[block].astype(F32)
        out = list(sums)
        for part in range(2):
            for i in range(ti):
                d_i = d_f[pl.ds(part * ti + i, ti, stride=2 * ti), :]
                for k in range(tj):
                    out[k] = out[k] + d_i * a_f[block, k, part, i : i + 1, :]
        return tuple(out)

    zero = tuple(jnp.zeros((ti, hid), F32) for _ in range(tj))
    grad_b = jnp.concatenate(lax.fori_loop(0, chips, backward_b, zero), 0) * mask

    send_da.wait_recv()
    grad_a = (da_f[:, core].reshape(tok, hid) + da_in[...]) * mask
    d_ga = (grad_a * val_a * sig_a * (1.0 - sig_a)).astype(BF16)
    d_va = (grad_a * sig_a).astype(BF16)
    d_x = d_x + dot_t(d_ga, wp_ref[:, :hid]) + dot_t(d_va, wp_ref[:, hid : 2 * hid])

    d_gb = (grad_b * val_b * sig_b * (1.0 - sig_b)).astype(BF16)
    d_vb = (grad_b * sig_b).astype(BF16)
    d_x = d_x + dot_t(d_gb, wp_ref[:, 2 * hid : 3 * hid]) + dot_t(d_vb, wp_ref[:, 3 * hid :])
    pair_grad = norm_back(d_x, hat_in, rstd_in, gin_ref[...])
    for k in range(tj):
        stage[pl.ds(k, ti, stride=tj), :] = pair_grad[k * ti : (k + 1) * ti, :]
    grad_ref[...] = stage[...].reshape(ti, tj, hid)

    for step in range(1, chips):
        send_b(step).wait_send()
        relay_a(step).wait_send()
    for step in range(chips):
        send_a(step).wait_send()
    send_go.wait_send()
    send_ol.wait_send()
    send_da.wait_send()
    for step in range(1, n_col):
        send_z(step).wait_send()
        block = flip(col, step, n_col)
        send_n(block).wait_send()
    for block in range(chips):
        @pl.when(block != col)
        def _():
            send_tri(block).wait_send()

    @pl.when(chip != col)
    def _():
        send_n(col).wait_send()


def store(upd_ref, grad_ref, upd_hbm, grad_hbm, sem):
    first = pltpu.make_async_copy(upd_ref, upd_hbm, sem.at[0])
    second = pltpu.make_async_copy(grad_ref, grad_hbm, sem.at[1])
    second.start()
    first.start()
    second.wait()
    first.wait()


def per_device(n_row, n_col, pair, pair_mask, gin, bin_, wp, bp, wg, bg, gmid, bmid, wo, bo, cot):
    ti, tj, chan = pair.shape
    hid = chan
    tok, half, chips = ti * tj, ti * ti, n_row // 2
    assert tj == 2 * ti and n_row == 2 * n_col
    vec = lambda v: v.reshape(1, -1)
    dma = pltpu.SemaphoreType.DMA
    vmem = pl.BlockSpec(memory_space=pltpu.VMEM)
    operands = (pair, pair_mask, vec(gin), vec(bin_), wp, vec(bp), wg, vec(bg), vec(gmid), vec(bmid), wo, vec(bo), cot)
    update, grad = pl.pallas_call(
        functools.partial(kernel, n_row, n_col, ti, tj),
        name="triangle_step",
        out_shape=(
            jax.ShapeDtypeStruct(pair.shape, BF16),
            jax.ShapeDtypeStruct(pair.shape, F32),
        ),
        in_specs=[pl.BlockSpec(memory_space=pltpu.HBM)] * 13,
        out_specs=(vmem, vmem),
        scratch_shapes=[pltpu.VMEM(v.shape, v.dtype) for v in operands]
        + [dma((len(operands),))]
        + [
            pltpu.VMEM((tok, hid), F32),
            pltpu.VMEM((tok, hid), BF16),
            pltpu.VMEM((chips, 2, tok, hid), BF16),
            pltpu.VMEM((chips, tj, 2, ti, hid), F32),
            pltpu.VMEM((tok, hid), BF16),
            pltpu.VMEM((chips, tok, hid), BF16),
            pltpu.VMEM((chips, tok, hid), F32),
            pltpu.VMEM((tok, hid), F32),
            pltpu.VMEM((n_col, tok, hid), BF16),
            pltpu.VMEM((n_col, tok, hid), BF16),
            pltpu.VMEM((2, half, hid), BF16),
            pltpu.VMEM((half, hid), BF16),
            pltpu.VMEM((ti, 2, ti, hid), F32),
            pltpu.VMEM((tok, hid), BF16),
            pltpu.VMEM((n_col, tok, hid), BF16),
            pltpu.VMEM((chips, tok, hid), BF16),
            pltpu.VMEM((tok, hid), F32),
            pltpu.VMEM((ti, 2, ti, hid), F32),
            pltpu.VMEM((half, hid), F32),
            pltpu.VMEM((2, half, hid), F32),
            pltpu.VMEM((tj, 2, ti, hid), F32),
            pltpu.VMEM((tok, hid), F32),
            pltpu.VMEM((tok, hid), F32),
            dma((chips,)),
            dma((chips, 2)),
            dma((chips,)),
            dma((chips,)),
            dma((chips,)),
            dma((n_col,)),
            dma((n_col,)),
            dma((n_col,)),
            dma((n_col,)),
            dma((n_col,)),
            dma((chips,)),
            dma((3,)),
            dma((3,)),
        ],
        compiler_params=pltpu.CompilerParams(
            collective_id=0, has_side_effects=True, vmem_limit_bytes=40 << 20
        ),
    )(*[pltpu.with_memory_space_constraint(v, pltpu.HBM) for v in operands])
    hbm = pl.BlockSpec(memory_space=pltpu.HBM)
    return pl.pallas_call(
        store,
        name="store_outputs",
        out_shape=(
            jax.ShapeDtypeStruct(pair.shape, BF16),
            jax.ShapeDtypeStruct(pair.shape, F32),
        ),
        in_specs=[vmem, vmem],
        out_specs=(hbm, hbm),
        scratch_shapes=[dma((2,))],
        compiler_params=pltpu.CompilerParams(vmem_limit_bytes=1 << 20),
    )(update, grad)


def solution(mesh):
    grid = P("row", "col", None)
    placed = (grid, P("row", "col")) + (P(),) * 10 + (grid,)
    return jax.shard_map(
        functools.partial(per_device, mesh.shape["row"], mesh.shape["col"]),
        mesh=mesh,
        in_specs=placed,
        out_specs=(grid, grid),
        check_vma=False,
    )
```

```python
import functools

import jax
import jax.numpy as jnp
from jax import lax
from jax.experimental import pallas as pl
from jax.experimental.pallas import tpu as pltpu
from jax.sharding import PartitionSpec as P

F32 = jnp.float32
BF16 = jnp.bfloat16
MESH = pl.DeviceIdType.MESH


def flip(index, step, size):
    if size & (size - 1):
        return lax.rem(index + step, size)
    partner, weight = 0, 1
    while weight < size:
        mine, other = (index // weight) % 2, (step // weight) % 2
        partner = partner + weight * ((mine + other) % 2)
        weight *= 2
    return partner


def source(index, step, size):
    if size & (size - 1):
        return lax.rem(index + size - step, size)
    return flip(index, step, size)


def normalize(values):
    centred = values - jnp.mean(values, -1, keepdims=True)
    inv_std = lax.rsqrt(jnp.mean(centred * centred, -1, keepdims=True) + 1e-05)
    return centred * inv_std, inv_std


def norm_back(upstream, hat, inv_std, gain):
    scaled = upstream * gain
    return inv_std * (
        scaled
        - jnp.mean(scaled, -1, keepdims=True)
        - hat * jnp.mean(scaled * hat, -1, keepdims=True)
    )


def dot(lhs, rhs):
    return jnp.dot(lhs, rhs, preferred_element_type=F32)


def dot_t(lhs, rhs):
    return lax.dot_general(lhs, rhs, (((1,), (1,)), ((), ())), preferred_element_type=F32)


def kernel(
    n_row, n_col, ti, tj,
    pair_hbm, mask_hbm, gin_hbm, bin_hbm, wp_hbm, bp_hbm, wg_hbm, bg_hbm,
    gmid_hbm, bmid_hbm, wo_hbm, bo_hbm, cot_hbm,
    upd_ref, grad_ref,
    pair_ref, mask_ref, gin_ref, bin_ref, wp_ref, bp_ref, wg_ref, bg_ref,
    gmid_ref, bmid_ref, wo_ref, bo_ref, cot_ref, in_sem,
    stage, a_out, a_in, a_f, b_out, b_in, b_f, tri_own, tri_out, tri_in,
    go_out, go_in, dm_f, d_out_s, dz_in, dn_in, d_f, ol_f, ol_out, ol_all, da_f, da_out, da_in,
    a_ss, a_rs, af_ss, b_ss, b_rs, t_ss, t_rs, z_ss, z_rs, n_ss, n_rs, c_ss, c_rs, ready,
):
    row, col = lax.axis_index("row"), lax.axis_index("col")
    chip, core = row // 2, row % 2
    partner = row + 1 - 2 * core
    tok = ti * tj
    half = ti * ti
    chips = n_row // 2
    hid = a_out.shape[-1]

    operands = (
        (pair_hbm, pair_ref), (wp_hbm, wp_ref), (gin_hbm, gin_ref), (bin_hbm, bin_ref),
        (bp_hbm, bp_ref), (mask_hbm, mask_ref), (wg_hbm, wg_ref), (bg_hbm, bg_ref),
        (cot_hbm, cot_ref), (wo_hbm, wo_ref), (gmid_hbm, gmid_ref), (bmid_hbm, bmid_ref),
        (bo_hbm, bo_ref),
    )
    loads = [
        pltpu.make_async_copy(src, dst, in_sem.at[n]) for n, (src, dst) in enumerate(operands)
    ]
    loads[0].start()
    barrier = pltpu.get_barrier_semaphore()

    def announce(to_row, to_col):
        pl.semaphore_signal(barrier, inc=1, device_id=(to_row, to_col), device_id_type=MESH)

    for step in reversed(range(1, chips)):
        announce(2 * flip(chip, step, chips), col)
    for step in reversed(range(1, n_col)):
        announce(2 * chip + 1, flip(col, step, n_col))
    announce(partner, col)
    for load in loads[1:]:
        load.start()

    def remote(src, dst, send, recv, to_row, to_col):
        return pltpu.make_async_remote_copy(
            src, dst, send, recv, device_id=(to_row, to_col), device_id_type=MESH
        )

    def reorder(ref):
        stage[...] = ref[...].astype(F32).reshape(tok, hid)
        return jnp.concatenate([stage[pl.ds(k, ti, stride=tj), :] for k in range(tj)], 0)

    loads[0].wait()
    hat_in, rstd_in = normalize(reorder(pair_ref))
    for load in loads[1:6]:
        load.wait()
    x_bf = (hat_in * gin_ref[...] + bin_ref[...]).astype(BF16)
    proj_b = dot(x_bf, wp_ref[:, 2 * hid :]) + bp_ref[:, 2 * hid :]
    mask_v = mask_ref[...].astype(F32)
    mask = jnp.concatenate(
        [jnp.broadcast_to(mask_v[:, k : k + 1], (ti, hid)) for k in range(tj)], 0
    )
    sig_b = jax.nn.sigmoid(proj_b[:, :hid])
    val_b = proj_b[:, hid:]
    b_bf = (mask * sig_b * val_b).astype(BF16)
    b_out[...] = b_bf

    @pl.when(core == 0)
    def _():
        pl.semaphore_wait(barrier, 2 * chips - 1)
        pl.semaphore_signal(ready, inc=1, device_id=(partner, col), device_id_type=MESH)

    @pl.when(core == 1)
    def _():
        pl.semaphore_wait(ready, 1)


    def send_b(step):
        to = flip(chip, step, chips)
        return remote(b_out, b_in.at[chip], b_ss.at[step], b_rs.at[chip], 2 * to + core, col)

    for step in reversed(range(1, chips)):
        send_b(step).start()

    proj_a = dot(x_bf, wp_ref[:, : 2 * hid]) + bp_ref[:, : 2 * hid]
    sig_a = jax.nn.sigmoid(proj_a[:, :hid])
    val_a = proj_a[:, hid:]
    a_bf = (mask * sig_a * val_a).astype(BF16)
    a_out[...] = a_bf

    def send_a(step):
        to = 2 * flip(chip, step, chips) + core if step else partner
        return remote(a_out, a_in.at[chip, core], a_ss.at[step], a_rs.at[chip, core], to, col)

    def relay_a(step):
        source_chip = source(chip, step, chips)
        held = a_in.at[source_chip, core]
        return remote(held, held, af_ss.at[source_chip], a_rs.at[source_chip, core], partner, col)

    def got_a(source_chip, source_core):
        return remote(
            a_out, a_in.at[source_chip, source_core], a_ss.at[0],
            a_rs.at[source_chip, source_core], partner, col,
        )

    for step in range(chips):
        send_a(step).start()
    a_f[chip, :, core] = a_bf.astype(F32).reshape(tj, ti, hid)
    b_f[chip] = b_bf.astype(F32)

    for load in loads[6:]:
        load.wait()
    gate = jax.nn.sigmoid(dot(x_bf, wg_ref[...]) + bg_ref[...])
    grad_out = reorder(cot_ref)
    go_out[...] = (grad_out * gate).astype(BF16).reshape(2, half, hid)
    send_go = remote(go_out.at[1 - core], go_in, c_ss.at[0], c_rs.at[0], partner, col)
    send_go.start()
    dm_f[:, core] = dot_t(go_out[core], wo_ref[...]).reshape(ti, ti, hid)

    def send_tri(block):
        return remote(
            tri_out.at[block], tri_in.at[col], t_ss.at[block], t_rs.at[col], row, block
        )

    def forward(block):
        sums = []
        a_k = [[a_f[chip, k, part] for part in range(2)] for k in range(tj)]
        for jj in range(ti):
            total = [None, None]
            for k in range(tj):
                b_row = b_f[block, k * ti + jj : k * ti + jj + 1, :]
                for part in range(2):
                    term = a_k[k][part] * b_row
                    total[part] = term if k == 0 else total[part] + term
            sums += total
        whole = jnp.concatenate(sums, 0)

        @pl.when(block == col)
        def _():
            tri_own[...] = whole

        @pl.when(block != col)
        def _():
            tri_out[block] = whole.astype(BF16)
            send_tri(block).start()

    @pl.when(core == 1)
    def _():
        pl.semaphore_wait(barrier, 2 * n_col - 1)
        pl.semaphore_signal(ready, inc=1, device_id=(partner, col), device_id_type=MESH)

    @pl.when(core == 0)
    def _():
        pl.semaphore_wait(ready, 1)

    got_a(chip, 1 - core).wait_recv()
    a_f[chip, :, 1 - core] = a_in[chip, 1 - core].astype(F32).reshape(tj, ti, hid)
    forward(chip)

    def forward_step(step, carry):
        block = source(chip, step, chips)
        remote(
            b_out, b_in.at[block], b_ss.at[step], b_rs.at[block], 2 * block + core, col
        ).wait_recv()
        b_f[block] = b_in[block].astype(F32)
        forward(block)
        return carry

    lax.fori_loop(1, chips, forward_step, 0)

    send_go.wait_recv()
    dm_f[:, 1 - core] = dot_t(go_in[...], wo_ref[...]).reshape(ti, ti, hid)
    scaled = dm_f[...].reshape(tok, hid) * gmid_ref[...]
    scaled = scaled - jnp.mean(scaled, -1, keepdims=True)

    for step in range(1, chips):
        source_chip = source(chip, step, chips)
        got_a(source_chip, core).wait_recv()
        relay_a(step).start()
        a_f[source_chip, :, core] = a_in[source_chip, core].astype(F32).reshape(tj, ti, hid)

    triangle = tri_own[...]
    for step in range(1, n_col):
        other = source(col, step, n_col)
        remote(
            tri_out.at[0], tri_in.at[other], t_ss.at[0], t_rs.at[other], row, other
        ).wait_recv()
        triangle = triangle + tri_in[other].astype(F32)
    centred = triangle - jnp.mean(triangle, -1, keepdims=True)
    variance = jnp.mean(centred * centred, -1, keepdims=True)
    slope = jnp.mean(scaled * centred, -1, keepdims=True)
    rstd_mid = lax.rsqrt(variance + 1e-05)
    hat_mid = centred * rstd_mid
    d_tri = (rstd_mid * (scaled - hat_mid * (rstd_mid * slope))).astype(BF16)
    d_out_s[...] = d_tri

    def send_z(step):
        to = flip(col, step, n_col)
        return remote(d_out_s, dz_in.at[col], z_ss.at[step], z_rs.at[col], row, to)

    def send_n(block):
        return remote(
            d_out_s, dn_in.at[chip], n_ss.at[block], n_rs.at[chip], 2 * col + core, block
        )

    for step in reversed(range(1, n_col)):
        send_z(step).start()
    for step in reversed(range(n_col)):
        block = flip(col, step, n_col)
        if step == 0:
            @pl.when(chip != col)
            def _():
                send_n(block).start()

            @pl.when(chip == col)
            def _():
                dn_in[chip] = d_tri
        else:
            send_n(block).start()

    mid_bf = (hat_mid * gmid_ref[...] + bmid_ref[...]).astype(BF16)
    ol_f[...] = (dot(mid_bf, wo_ref[...]) + bo_ref[...]).reshape(ti, 2, ti, hid)
    ol_out[...] = ol_f[:, 1 - core].reshape(half, hid)
    send_ol = remote(ol_out, ol_all.at[core], c_ss.at[1], c_rs.at[1], partner, col)
    send_ol.start()
    ol_all[core] = ol_f[:, core].reshape(half, hid)

    def backward_a(block, d_block, sums):
        out = list(sums)
        for jj in range(ti):
            d_j = [d_block[(2 * jj + part) * ti : (2 * jj + part + 1) * ti] for part in range(2)]
            for k in range(tj):
                b_row = b_f[block, k * ti + jj : k * ti + jj + 1, :]
                for part in range(2):
                    out[2 * k + part] = out[2 * k + part] + d_j[part] * b_row
        return tuple(out)

    zero = tuple(jnp.zeros((ti, hid), F32) for _ in range(2 * tj))
    sums_a = backward_a(col, d_tri.astype(F32), zero)

    for step in range(1, chips):
        source_chip = source(chip, step, chips)
        got_a(source_chip, 1 - core).wait_recv()
        a_f[source_chip, :, 1 - core] = a_in[source_chip, 1 - core].astype(F32).reshape(tj, ti, hid)

    send_ol.wait_recv()
    out_lin = ol_all[...].reshape(tok, hid)
    update = gate * out_lin
    for k in range(tj):
        stage[pl.ds(k, ti, stride=tj), :] = update[k * ti : (k + 1) * ti, :]
    upd_ref[...] = stage[...].astype(BF16).reshape(ti, tj, hid)
    d_gpre = (grad_out * out_lin * gate * (1.0 - gate)).astype(BF16)
    d_x = dot_t(d_gpre, wg_ref[...])

    def backward_step(step, sums):
        other = source(col, step, n_col)
        remote(
            d_out_s, dz_in.at[other], z_ss.at[step], z_rs.at[other], row, other
        ).wait_recv()
        return backward_a(other, dz_in[other].astype(F32), sums)

    sums_a = lax.fori_loop(1, n_col, backward_step, sums_a)
    da_f[...] = jnp.concatenate(sums_a, 0).reshape(tj, 2, ti, hid)
    da_out[...] = da_f[:, 1 - core].reshape(tok, hid)
    send_da = remote(da_out, da_in, c_ss.at[2], c_rs.at[2], partner, col)
    send_da.start()

    def backward_b(step, sums):
        block = source(chip, step, chips)

        @pl.when(jnp.logical_or(block != chip, chip != col))
        def _():
            remote(
                d_out_s, dn_in.at[block], n_ss.at[0], n_rs.at[block], 2 * block + core, chip
            ).wait_recv()

        d_f[...] = dn_in[block].astype(F32)
        out = list(sums)
        for part in range(2):
            for i in range(ti):
                d_i = d_f[pl.ds(part * ti + i, ti, stride=2 * ti), :]
                for k in range(tj):
                    out[k] = out[k] + d_i * a_f[block, k, part, i : i + 1, :]
        return tuple(out)

    zero = tuple(jnp.zeros((ti, hid), F32) for _ in range(tj))
    grad_b = jnp.concatenate(lax.fori_loop(0, chips, backward_b, zero), 0) * mask

    send_da.wait_recv()
    grad_a = (da_f[:, core].reshape(tok, hid) + da_in[...]) * mask
    d_ga = (grad_a * val_a * sig_a * (1.0 - sig_a)).astype(BF16)
    d_va = (grad_a * sig_a).astype(BF16)
    d_x = d_x + dot_t(d_ga, wp_ref[:, :hid]) + dot_t(d_va, wp_ref[:, hid : 2 * hid])

    d_gb = (grad_b * val_b * sig_b * (1.0 - sig_b)).astype(BF16)
    d_vb = (grad_b * sig_b).astype(BF16)
    d_x = d_x + dot_t(d_gb, wp_ref[:, 2 * hid : 3 * hid]) + dot_t(d_vb, wp_ref[:, 3 * hid :])
    pair_grad = norm_back(d_x, hat_in, rstd_in, gin_ref[...])
    for k in range(tj):
        stage[pl.ds(k, ti, stride=tj), :] = pair_grad[k * ti : (k + 1) * ti, :]
    grad_ref[...] = stage[...].reshape(ti, tj, hid)

    for step in range(1, chips):
        send_b(step).wait_send()
        relay_a(step).wait_send()
    for step in range(chips):
        send_a(step).wait_send()
    send_go.wait_send()
    send_ol.wait_send()
    send_da.wait_send()
    for step in range(1, n_col):
        send_z(step).wait_send()
        block = flip(col, step, n_col)
        send_n(block).wait_send()
    for block in range(chips):
        @pl.when(block != col)
        def _():
            send_tri(block).wait_send()

    @pl.when(chip != col)
    def _():
        send_n(col).wait_send()


def store(upd_ref, grad_ref, upd_hbm, grad_hbm, sem):
    first = pltpu.make_async_copy(upd_ref, upd_hbm, sem.at[0])
    second = pltpu.make_async_copy(grad_ref, grad_hbm, sem.at[1])
    second.start()
    first.start()
    second.wait()
    first.wait()


def per_device(n_row, n_col, pair, pair_mask, gin, bin_, wp, bp, wg, bg, gmid, bmid, wo, bo, cot):
    ti, tj, chan = pair.shape
    hid = chan
    tok, half, chips = ti * tj, ti * ti, n_row // 2
    assert tj == 2 * ti and n_row == 2 * n_col
    vec = lambda v: v.reshape(1, -1)
    dma = pltpu.SemaphoreType.DMA
    vmem = pl.BlockSpec(memory_space=pltpu.VMEM)
    operands = (pair, pair_mask, vec(gin), vec(bin_), wp, vec(bp), wg, vec(bg), vec(gmid), vec(bmid), wo, vec(bo), cot)
    update, grad = pl.pallas_call(
        functools.partial(kernel, n_row, n_col, ti, tj),
        name="triangle_step",
        out_shape=(
            jax.ShapeDtypeStruct(pair.shape, BF16),
            jax.ShapeDtypeStruct(pair.shape, F32),
        ),
        in_specs=[pl.BlockSpec(memory_space=pltpu.HBM)] * 13,
        out_specs=(vmem, vmem),
        scratch_shapes=[pltpu.VMEM(v.shape, v.dtype) for v in operands]
        + [dma((len(operands),))]
        + [
            pltpu.VMEM((tok, hid), F32),
            pltpu.VMEM((tok, hid), BF16),
            pltpu.VMEM((chips, 2, tok, hid), BF16),
            pltpu.VMEM((chips, tj, 2, ti, hid), F32),
            pltpu.VMEM((tok, hid), BF16),
            pltpu.VMEM((chips, tok, hid), BF16),
            pltpu.VMEM((chips, tok, hid), F32),
            pltpu.VMEM((tok, hid), F32),
            pltpu.VMEM((n_col, tok, hid), BF16),
            pltpu.VMEM((n_col, tok, hid), BF16),
            pltpu.VMEM((2, half, hid), BF16),
            pltpu.VMEM((half, hid), BF16),
            pltpu.VMEM((ti, 2, ti, hid), F32),
            pltpu.VMEM((tok, hid), BF16),
            pltpu.VMEM((n_col, tok, hid), BF16),
            pltpu.VMEM((chips, tok, hid), BF16),
            pltpu.VMEM((tok, hid), F32),
            pltpu.VMEM((ti, 2, ti, hid), F32),
            pltpu.VMEM((half, hid), F32),
            pltpu.VMEM((2, half, hid), F32),
            pltpu.VMEM((tj, 2, ti, hid), F32),
            pltpu.VMEM((tok, hid), F32),
            pltpu.VMEM((tok, hid), F32),
            dma((chips,)),
            dma((chips, 2)),
            dma((chips,)),
            dma((chips,)),
            dma((chips,)),
            dma((n_col,)),
            dma((n_col,)),
            dma((n_col,)),
            dma((n_col,)),
            dma((n_col,)),
            dma((chips,)),
            dma((3,)),
            dma((3,)),
            pltpu.SemaphoreType.REGULAR,
        ],
        compiler_params=pltpu.CompilerParams(
            collective_id=0, has_side_effects=True, vmem_limit_bytes=40 << 20
        ),
    )(*[pltpu.with_memory_space_constraint(v, pltpu.HBM) for v in operands])
    hbm = pl.BlockSpec(memory_space=pltpu.HBM)
    return pl.pallas_call(
        store,
        name="store_outputs",
        out_shape=(
            jax.ShapeDtypeStruct(pair.shape, BF16),
            jax.ShapeDtypeStruct(pair.shape, F32),
        ),
        in_specs=[vmem, vmem],
        out_specs=(hbm, hbm),
        scratch_shapes=[dma((2,))],
        compiler_params=pltpu.CompilerParams(vmem_limit_bytes=1 << 20),
    )(update, grad)


def solution(mesh):
    grid = P("row", "col", None)
    placed = (grid, P("row", "col")) + (P(),) * 10 + (grid,)
    return jax.shard_map(
        functools.partial(per_device, mesh.shape["row"], mesh.shape["col"]),
        mesh=mesh,
        in_specs=placed,
        out_specs=(grid, grid),
        check_vma=False,
    )
```

```python
import functools

import jax
import jax.numpy as jnp
from jax import lax
from jax.experimental import pallas as pl
from jax.experimental.pallas import tpu as pltpu
from jax.sharding import PartitionSpec as P

F32 = jnp.float32
BF16 = jnp.bfloat16
MESH = pl.DeviceIdType.MESH


def flip(index, step, size):
    if size & (size - 1):
        return lax.rem(index + step, size)
    partner, weight = 0, 1
    while weight < size:
        mine, other = (index // weight) % 2, (step // weight) % 2
        partner = partner + weight * ((mine + other) % 2)
        weight *= 2
    return partner


def source(index, step, size):
    if size & (size - 1):
        return lax.rem(index + size - step, size)
    return flip(index, step, size)


def normalize(values):
    centred = values - jnp.mean(values, -1, keepdims=True)
    inv_std = lax.rsqrt(jnp.mean(centred * centred, -1, keepdims=True) + 1e-05)
    return centred * inv_std, inv_std


def norm_back(upstream, hat, inv_std, gain):
    scaled = upstream * gain
    return inv_std * (
        scaled
        - jnp.mean(scaled, -1, keepdims=True)
        - hat * jnp.mean(scaled * hat, -1, keepdims=True)
    )


def dot(lhs, rhs):
    return jnp.dot(lhs, rhs, preferred_element_type=F32)


def dot_t(lhs, rhs):
    return lax.dot_general(lhs, rhs, (((1,), (1,)), ((), ())), preferred_element_type=F32)


def kernel(
    n_row, n_col, ti, tj,
    pair_hbm, mask_hbm, gin_hbm, bin_hbm, wp_hbm, bp_hbm, wg_hbm, bg_hbm,
    gmid_hbm, bmid_hbm, wo_hbm, bo_hbm, cot_hbm,
    upd_ref, grad_ref,
    pair_ref, mask_ref, gin_ref, bin_ref, wp_ref, bp_ref, wg_ref, bg_ref,
    gmid_ref, bmid_ref, wo_ref, bo_ref, cot_ref, in_sem,
    stage, a_out, a_in, a_f, b_out, b_in, b_f, tri_own, tri_out, tri_in,
    go_out, go_in, dm_f, d_out_s, dz_in, dn_in, d_f, ol_f, ol_out, ol_all, da_f, da_out, da_in,
    a_ss, a_rs, af_ss, b_ss, b_rs, t_ss, t_rs, z_ss, z_rs, n_ss, n_rs, c_ss, c_rs, ready,
):
    row, col = lax.axis_index("row"), lax.axis_index("col")
    chip, core = row // 2, row % 2
    partner = row + 1 - 2 * core
    tok = ti * tj
    half = ti * ti
    chips = n_row // 2
    hid = a_out.shape[-1]

    operands = (
        (pair_hbm, pair_ref), (wp_hbm, wp_ref), (gin_hbm, gin_ref), (bin_hbm, bin_ref),
        (bp_hbm, bp_ref), (mask_hbm, mask_ref), (wg_hbm, wg_ref), (bg_hbm, bg_ref),
        (cot_hbm, cot_ref), (wo_hbm, wo_ref), (gmid_hbm, gmid_ref), (bmid_hbm, bmid_ref),
        (bo_hbm, bo_ref),
    )
    loads = [
        pltpu.make_async_copy(src, dst, in_sem.at[n]) for n, (src, dst) in enumerate(operands)
    ]
    loads[0].start()
    barrier = pltpu.get_barrier_semaphore()

    def announce(to_row, to_col):
        pl.semaphore_signal(barrier, inc=1, device_id=(to_row, to_col), device_id_type=MESH)

    for step in reversed(range(1, chips)):
        announce(2 * flip(chip, step, chips) + 1, col)
    for step in reversed(range(1, n_col)):
        announce(2 * chip, flip(col, step, n_col))
    announce(partner, col)
    for load in loads[1:]:
        load.start()

    def remote(src, dst, send, recv, to_row, to_col):
        return pltpu.make_async_remote_copy(
            src, dst, send, recv, device_id=(to_row, to_col), device_id_type=MESH
        )

    def reorder(ref):
        stage[...] = ref[...].astype(F32).reshape(tok, hid)
        return jnp.concatenate([stage[pl.ds(k, ti, stride=tj), :] for k in range(tj)], 0)

    loads[0].wait()
    hat_in, rstd_in = normalize(reorder(pair_ref))
    for load in loads[1:6]:
        load.wait()
    x_bf = (hat_in * gin_ref[...] + bin_ref[...]).astype(BF16)
    proj_b = dot(x_bf, wp_ref[:, 2 * hid :]) + bp_ref[:, 2 * hid :]
    mask_v = mask_ref[...].astype(F32)
    mask = jnp.concatenate(
        [jnp.broadcast_to(mask_v[:, k : k + 1], (ti, hid)) for k in range(tj)], 0
    )
    sig_b = jax.nn.sigmoid(proj_b[:, :hid])
    val_b = proj_b[:, hid:]
    b_bf = (mask * sig_b * val_b).astype(BF16)
    b_out[...] = b_bf

    @pl.when(core == 1)
    def _():
        pl.semaphore_wait(barrier, 2 * chips - 1)
        pl.semaphore_signal(ready, inc=1, device_id=(partner, col), device_id_type=MESH)

    @pl.when(core == 0)
    def _():
        pl.semaphore_wait(ready, 1)


    def send_b(step):
        to = flip(chip, step, chips)
        return remote(b_out, b_in.at[chip], b_ss.at[step], b_rs.at[chip], 2 * to + core, col)

    for step in range(1, chips):
        send_b(step).start()

    proj_a = dot(x_bf, wp_ref[:, : 2 * hid]) + bp_ref[:, : 2 * hid]
    sig_a = jax.nn.sigmoid(proj_a[:, :hid])
    val_a = proj_a[:, hid:]
    a_bf = (mask * sig_a * val_a).astype(BF16)
    a_out[...] = a_bf

    def send_a(step):
        to = 2 * flip(chip, step, chips) + core if step else partner
        return remote(a_out, a_in.at[chip, core], a_ss.at[step], a_rs.at[chip, core], to, col)

    def relay_a(step):
        source_chip = source(chip, step, chips)
        held = a_in.at[source_chip, core]
        return remote(held, held, af_ss.at[source_chip], a_rs.at[source_chip, core], partner, col)

    def got_a(source_chip, source_core):
        return remote(
            a_out, a_in.at[source_chip, source_core], a_ss.at[0],
            a_rs.at[source_chip, source_core], partner, col,
        )

    for step in range(chips):
        send_a(step).start()
    a_f[chip, :, core] = a_bf.astype(F32).reshape(tj, ti, hid)
    b_f[chip] = b_bf.astype(F32)

    for load in loads[6:]:
        load.wait()
    gate = jax.nn.sigmoid(dot(x_bf, wg_ref[...]) + bg_ref[...])
    grad_out = reorder(cot_ref)
    go_out[...] = (grad_out * gate).astype(BF16).reshape(2, half, hid)
    send_go = remote(go_out.at[1 - core], go_in, c_ss.at[0], c_rs.at[0], partner, col)
    send_go.start()
    dm_f[:, core] = dot_t(go_out[core], wo_ref[...]).reshape(ti, ti, hid)

    def send_tri(block):
        return remote(
            tri_out.at[block], tri_in.at[col], t_ss.at[block], t_rs.at[col], row, block
        )

    def forward(block):
        sums = []
        a_k = [[a_f[chip, k, part] for part in range(2)] for k in range(tj)]
        for jj in range(ti):
            total = [None, None]
            for k in range(tj):
                b_row = b_f[block, k * ti + jj : k * ti + jj + 1, :]
                for part in range(2):
                    term = a_k[k][part] * b_row
                    total[part] = term if k == 0 else total[part] + term
            sums += total
        whole = jnp.concatenate(sums, 0)

        @pl.when(block == col)
        def _():
            tri_own[...] = whole

        @pl.when(block != col)
        def _():
            tri_out[block] = whole.astype(BF16)
            send_tri(block).start()

    @pl.when(core == 0)
    def _():
        pl.semaphore_wait(barrier, 2 * n_col - 1)
        pl.semaphore_signal(ready, inc=1, device_id=(partner, col), device_id_type=MESH)

    @pl.when(core == 1)
    def _():
        pl.semaphore_wait(ready, 1)

    got_a(chip, 1 - core).wait_recv()
    a_f[chip, :, 1 - core] = a_in[chip, 1 - core].astype(F32).reshape(tj, ti, hid)
    forward(chip)

    def forward_step(step, carry):
        block = source(chip, step, chips)
        remote(
            b_out, b_in.at[block], b_ss.at[step], b_rs.at[block], 2 * block + core, col
        ).wait_recv()
        b_f[block] = b_in[block].astype(F32)
        forward(block)
        return carry

    lax.fori_loop(1, chips, forward_step, 0)

    send_go.wait_recv()
    dm_f[:, 1 - core] = dot_t(go_in[...], wo_ref[...]).reshape(ti, ti, hid)
    scaled = dm_f[...].reshape(tok, hid) * gmid_ref[...]
    scaled = scaled - jnp.mean(scaled, -1, keepdims=True)

    for step in range(1, chips):
        source_chip = source(chip, step, chips)
        got_a(source_chip, core).wait_recv()
        relay_a(step).start()
        a_f[source_chip, :, core] = a_in[source_chip, core].astype(F32).reshape(tj, ti, hid)

    triangle = tri_own[...]
    for step in range(1, n_col):
        other = source(col, step, n_col)
        remote(
            tri_out.at[0], tri_in.at[other], t_ss.at[0], t_rs.at[other], row, other
        ).wait_recv()
        triangle = triangle + tri_in[other].astype(F32)
    centred = triangle - jnp.mean(triangle, -1, keepdims=True)
    variance = jnp.mean(centred * centred, -1, keepdims=True)
    slope = jnp.mean(scaled * centred, -1, keepdims=True)
    rstd_mid = lax.rsqrt(variance + 1e-05)
    hat_mid = centred * rstd_mid
    d_tri = (rstd_mid * (scaled - hat_mid * (rstd_mid * slope))).astype(BF16)
    d_out_s[...] = d_tri

    dz_in[col] = d_tri

    def send_z(block):
        return remote(d_out_s, dz_in.at[col], z_ss.at[block], z_rs.at[col], row, block)

    def send_n(block):
        return remote(
            d_out_s, dn_in.at[chip], n_ss.at[block], n_rs.at[chip], 2 * col + core, block
        )

    for block in range(n_col):
        @pl.when(block != col)
        def _():
            send_z(block).start()

        @pl.when(chip != col)
        def _():
            send_n(block).start()

    mid_bf = (hat_mid * gmid_ref[...] + bmid_ref[...]).astype(BF16)
    ol_f[...] = (dot(mid_bf, wo_ref[...]) + bo_ref[...]).reshape(ti, 2, ti, hid)
    ol_out[...] = ol_f[:, 1 - core].reshape(half, hid)
    send_ol = remote(ol_out, ol_all.at[core], c_ss.at[1], c_rs.at[1], partner, col)
    send_ol.start()
    ol_all[core] = ol_f[:, core].reshape(half, hid)

    def backward_a(block, d_block, sums):
        out = list(sums)
        for jj in range(ti):
            d_j = [d_block[(2 * jj + part) * ti : (2 * jj + part + 1) * ti] for part in range(2)]
            for k in range(tj):
                b_row = b_f[block, k * ti + jj : k * ti + jj + 1, :]
                for part in range(2):
                    out[2 * k + part] = out[2 * k + part] + d_j[part] * b_row
        return tuple(out)

    zero = tuple(jnp.zeros((ti, hid), F32) for _ in range(2 * tj))
    sums_a = backward_a(col, d_tri.astype(F32), zero)

    for step in range(1, chips):
        source_chip = source(chip, step, chips)
        got_a(source_chip, 1 - core).wait_recv()
        a_f[source_chip, :, 1 - core] = a_in[source_chip, 1 - core].astype(F32).reshape(tj, ti, hid)

    send_ol.wait_recv()
    out_lin = ol_all[...].reshape(tok, hid)
    update = gate * out_lin
    for k in range(tj):
        stage[pl.ds(k, ti, stride=tj), :] = update[k * ti : (k + 1) * ti, :]
    upd_ref[...] = stage[...].astype(BF16).reshape(ti, tj, hid)
    d_gpre = (grad_out * out_lin * gate * (1.0 - gate)).astype(BF16)
    d_x = dot_t(d_gpre, wg_ref[...])

    def backward_step(step, sums):
        other = source(col, step, n_col)
        remote(
            d_out_s, dz_in.at[other], z_ss.at[0], z_rs.at[other], row, other
        ).wait_recv()
        return backward_a(other, dz_in[other].astype(F32), sums)

    sums_a = lax.fori_loop(1, n_col, backward_step, sums_a)
    da_f[...] = jnp.concatenate(sums_a, 0).reshape(tj, 2, ti, hid)
    da_out[...] = da_f[:, 1 - core].reshape(tok, hid)
    send_da = remote(da_out, da_in, c_ss.at[2], c_rs.at[2], partner, col)
    send_da.start()

    def backward_b(block, d_block, sums):
        d_f[...] = d_block.astype(F32)
        out = list(sums)
        for part in range(2):
            for i in range(ti):
                d_i = d_f[pl.ds(part * ti + i, ti, stride=2 * ti), :]
                for k in range(tj):
                    out[k] = out[k] + d_i * a_f[block, k, part, i : i + 1, :]
        return tuple(out)

    def backward_b_step(step, sums):
        block = source(chip, step, chips)
        remote(
            d_out_s, dn_in.at[block], n_ss.at[0], n_rs.at[block], 2 * block + core, chip
        ).wait_recv()
        return backward_b(block, dn_in[block], sums)

    zero = tuple(jnp.zeros((ti, hid), F32) for _ in range(tj))
    sums_b = backward_b(chip, dz_in[chip], zero)
    sums_b = lax.fori_loop(1, chips, backward_b_step, sums_b)
    grad_b = jnp.concatenate(sums_b, 0) * mask

    send_da.wait_recv()
    grad_a = (da_f[:, core].reshape(tok, hid) + da_in[...]) * mask
    d_ga = (grad_a * val_a * sig_a * (1.0 - sig_a)).astype(BF16)
    d_va = (grad_a * sig_a).astype(BF16)
    d_x = d_x + dot_t(d_ga, wp_ref[:, :hid]) + dot_t(d_va, wp_ref[:, hid : 2 * hid])

    d_gb = (grad_b * val_b * sig_b * (1.0 - sig_b)).astype(BF16)
    d_vb = (grad_b * sig_b).astype(BF16)
    d_x = d_x + dot_t(d_gb, wp_ref[:, 2 * hid : 3 * hid]) + dot_t(d_vb, wp_ref[:, 3 * hid :])
    pair_grad = norm_back(d_x, hat_in, rstd_in, gin_ref[...])
    for k in range(tj):
        stage[pl.ds(k, ti, stride=tj), :] = pair_grad[k * ti : (k + 1) * ti, :]
    grad_ref[...] = stage[...].reshape(ti, tj, hid)

    for step in range(1, chips):
        send_b(step).wait_send()
        relay_a(step).wait_send()
    for step in range(chips):
        send_a(step).wait_send()
    send_go.wait_send()
    send_ol.wait_send()
    send_da.wait_send()
    for block in range(n_col):
        @pl.when(block != col)
        def _():
            send_tri(block).wait_send()
            send_z(block).wait_send()

        @pl.when(chip != col)
        def _():
            send_n(block).wait_send()


def store(upd_ref, grad_ref, upd_hbm, grad_hbm, sem):
    first = pltpu.make_async_copy(upd_ref, upd_hbm, sem.at[0])
    second = pltpu.make_async_copy(grad_ref, grad_hbm, sem.at[1])
    second.start()
    first.start()
    second.wait()
    first.wait()


def per_device(n_row, n_col, pair, pair_mask, gin, bin_, wp, bp, wg, bg, gmid, bmid, wo, bo, cot):
    ti, tj, chan = pair.shape
    hid = chan
    tok, half, chips = ti * tj, ti * ti, n_row // 2
    assert tj == 2 * ti and n_row == 2 * n_col
    vec = lambda v: v.reshape(1, -1)
    dma = pltpu.SemaphoreType.DMA
    vmem = pl.BlockSpec(memory_space=pltpu.VMEM)
    operands = (pair, pair_mask, vec(gin), vec(bin_), wp, vec(bp), wg, vec(bg), vec(gmid), vec(bmid), wo, vec(bo), cot)
    update, grad = pl.pallas_call(
        functools.partial(kernel, n_row, n_col, ti, tj),
        name="triangle_step",
        out_shape=(
            jax.ShapeDtypeStruct(pair.shape, BF16),
            jax.ShapeDtypeStruct(pair.shape, F32),
        ),
        in_specs=[pl.BlockSpec(memory_space=pltpu.HBM)] * 13,
        out_specs=(vmem, vmem),
        scratch_shapes=[pltpu.VMEM(v.shape, v.dtype) for v in operands]
        + [dma((len(operands),))]
        + [
            pltpu.VMEM((tok, hid), F32),
            pltpu.VMEM((tok, hid), BF16),
            pltpu.VMEM((chips, 2, tok, hid), BF16),
            pltpu.VMEM((chips, tj, 2, ti, hid), F32),
            pltpu.VMEM((tok, hid), BF16),
            pltpu.VMEM((chips, tok, hid), BF16),
            pltpu.VMEM((chips, tok, hid), F32),
            pltpu.VMEM((tok, hid), F32),
            pltpu.VMEM((n_col, tok, hid), BF16),
            pltpu.VMEM((n_col, tok, hid), BF16),
            pltpu.VMEM((2, half, hid), BF16),
            pltpu.VMEM((half, hid), BF16),
            pltpu.VMEM((ti, 2, ti, hid), F32),
            pltpu.VMEM((tok, hid), BF16),
            pltpu.VMEM((n_col, tok, hid), BF16),
            pltpu.VMEM((chips, tok, hid), BF16),
            pltpu.VMEM((tok, hid), F32),
            pltpu.VMEM((ti, 2, ti, hid), F32),
            pltpu.VMEM((half, hid), F32),
            pltpu.VMEM((2, half, hid), F32),
            pltpu.VMEM((tj, 2, ti, hid), F32),
            pltpu.VMEM((tok, hid), F32),
            pltpu.VMEM((tok, hid), F32),
            dma((chips,)),
            dma((chips, 2)),
            dma((chips,)),
            dma((chips,)),
            dma((chips,)),
            dma((n_col,)),
            dma((n_col,)),
            dma((n_col,)),
            dma((n_col,)),
            dma((n_col,)),
            dma((chips,)),
            dma((3,)),
            dma((3,)),
            pltpu.SemaphoreType.REGULAR,
        ],
        compiler_params=pltpu.CompilerParams(
            collective_id=0, has_side_effects=True, vmem_limit_bytes=40 << 20
        ),
    )(*[pltpu.with_memory_space_constraint(v, pltpu.HBM) for v in operands])
    hbm = pl.BlockSpec(memory_space=pltpu.HBM)
    return pl.pallas_call(
        store,
        name="store_outputs",
        out_shape=(
            jax.ShapeDtypeStruct(pair.shape, BF16),
            jax.ShapeDtypeStruct(pair.shape, F32),
        ),
        in_specs=[vmem, vmem],
        out_specs=(hbm, hbm),
        scratch_shapes=[dma((2,))],
        compiler_params=pltpu.CompilerParams(vmem_limit_bytes=1 << 20),
    )(update, grad)


def solution(mesh):
    grid = P("row", "col", None)
    placed = (grid, P("row", "col")) + (P(),) * 10 + (grid,)
    return jax.shard_map(
        functools.partial(per_device, mesh.shape["row"], mesh.shape["col"]),
        mesh=mesh,
        in_specs=placed,
        out_specs=(grid, grid),
        check_vma=False,
    )
```

```python
import functools

import jax
import jax.numpy as jnp
from jax import lax
from jax.experimental import pallas as pl
from jax.experimental.pallas import tpu as pltpu
from jax.sharding import PartitionSpec as P

F32 = jnp.float32
BF16 = jnp.bfloat16
MESH = pl.DeviceIdType.MESH


def flip(index, step, size):
    if size & (size - 1):
        return lax.rem(index + step, size)
    partner, weight = 0, 1
    while weight < size:
        mine, other = (index // weight) % 2, (step // weight) % 2
        partner = partner + weight * ((mine + other) % 2)
        weight *= 2
    return partner


def source(index, step, size):
    if size & (size - 1):
        return lax.rem(index + size - step, size)
    return flip(index, step, size)


def normalize(values):
    centred = values - jnp.mean(values, -1, keepdims=True)
    inv_std = lax.rsqrt(jnp.mean(centred * centred, -1, keepdims=True) + 1e-05)
    return centred * inv_std, inv_std


def norm_back(upstream, hat, inv_std, gain):
    scaled = upstream * gain
    return inv_std * (
        scaled
        - jnp.mean(scaled, -1, keepdims=True)
        - hat * jnp.mean(scaled * hat, -1, keepdims=True)
    )


def dot(lhs, rhs):
    return jnp.dot(lhs, rhs, preferred_element_type=F32)


def dot_t(lhs, rhs):
    return lax.dot_general(lhs, rhs, (((1,), (1,)), ((), ())), preferred_element_type=F32)


def kernel(
    n_row, n_col, ti, tj,
    pair_hbm, mask_hbm, gin_hbm, bin_hbm, wp_hbm, bp_hbm, wg_hbm, bg_hbm,
    gmid_hbm, bmid_hbm, wo_hbm, bo_hbm, cot_hbm,
    upd_ref, grad_ref,
    pair_ref, mask_ref, gin_ref, bin_ref, wp_ref, bp_ref, wg_ref, bg_ref,
    gmid_ref, bmid_ref, wo_ref, bo_ref, cot_ref, in_sem,
    stage, a_out, a_in, a_f, b_out, b_in, b_f, tri_own, tri_out, tri_in,
    go_out, go_in, dm_f, d_out_s, dz_in, dn_in, d_f, ol_f, ol_out, ol_all, da_f, da_out, da_in,
    a_ss, a_rs, af_ss, b_ss, b_rs, t_ss, t_rs, z_ss, z_rs, n_ss, n_rs, c_ss, c_rs, ready,
):
    row, col = lax.axis_index("row"), lax.axis_index("col")
    chip, core = row // 2, row % 2
    partner = row + 1 - 2 * core
    tok = ti * tj
    half = ti * ti
    chips = n_row // 2
    hid = a_out.shape[-1]

    operands = (
        (pair_hbm, pair_ref), (wp_hbm, wp_ref), (gin_hbm, gin_ref), (bin_hbm, bin_ref),
        (bp_hbm, bp_ref), (mask_hbm, mask_ref), (wg_hbm, wg_ref), (bg_hbm, bg_ref),
        (cot_hbm, cot_ref), (wo_hbm, wo_ref), (gmid_hbm, gmid_ref), (bmid_hbm, bmid_ref),
        (bo_hbm, bo_ref),
    )
    loads = [
        pltpu.make_async_copy(src, dst, in_sem.at[n]) for n, (src, dst) in enumerate(operands)
    ]
    loads[0].start()
    barrier = pltpu.get_barrier_semaphore()

    def announce(to_row, to_col):
        pl.semaphore_signal(barrier, inc=1, device_id=(to_row, to_col), device_id_type=MESH)

    for step in reversed(range(1, chips)):
        announce(2 * flip(chip, step, chips) + 1, col)
    for step in reversed(range(1, n_col)):
        announce(2 * chip, flip(col, step, n_col))
    announce(partner, col)
    for load in loads[1:]:
        load.start()

    def remote(src, dst, send, recv, to_row, to_col):
        return pltpu.make_async_remote_copy(
            src, dst, send, recv, device_id=(to_row, to_col), device_id_type=MESH
        )

    def reorder(ref):
        stage[...] = ref[...].astype(F32).reshape(tok, hid)
        return jnp.concatenate([stage[pl.ds(k, ti, stride=tj), :] for k in range(tj)], 0)

    loads[0].wait()
    hat_in, rstd_in = normalize(reorder(pair_ref))
    for load in loads[1:6]:
        load.wait()
    x_bf = (hat_in * gin_ref[...] + bin_ref[...]).astype(BF16)
    proj_b = dot(x_bf, wp_ref[:, 2 * hid :]) + bp_ref[:, 2 * hid :]
    mask_v = mask_ref[...].astype(F32)
    mask = jnp.concatenate(
        [jnp.broadcast_to(mask_v[:, k : k + 1], (ti, hid)) for k in range(tj)], 0
    )
    sig_b = jax.nn.sigmoid(proj_b[:, :hid])
    val_b = proj_b[:, hid:]
    b_bf = (mask * sig_b * val_b).astype(BF16)
    b_out[...] = b_bf

    @pl.when(core == 1)
    def _():
        pl.semaphore_wait(barrier, 2 * chips - 1)
        pl.semaphore_signal(ready, inc=1, device_id=(partner, col), device_id_type=MESH)

    @pl.when(core == 0)
    def _():
        pl.semaphore_wait(ready, 1)


    def send_b(to):
        return remote(b_out, b_in.at[chip], b_ss.at[to], b_rs.at[chip], 2 * to + core, col)

    for to in range(chips):
        @pl.when(to != chip)
        def _():
            send_b(to).start()

    proj_a = dot(x_bf, wp_ref[:, : 2 * hid]) + bp_ref[:, : 2 * hid]
    sig_a = jax.nn.sigmoid(proj_a[:, :hid])
    val_a = proj_a[:, hid:]
    a_bf = (mask * sig_a * val_a).astype(BF16)
    a_out[...] = a_bf

    def send_a(step):
        to = 2 * flip(chip, step, chips) + core if step else partner
        return remote(a_out, a_in.at[chip, core], a_ss.at[step], a_rs.at[chip, core], to, col)

    def relay_a(step):
        source_chip = source(chip, step, chips)
        held = a_in.at[source_chip, core]
        return remote(held, held, af_ss.at[source_chip], a_rs.at[source_chip, core], partner, col)

    def got_a(source_chip, source_core):
        return remote(
            a_out, a_in.at[source_chip, source_core], a_ss.at[0],
            a_rs.at[source_chip, source_core], partner, col,
        )

    for step in range(chips):
        send_a(step).start()
    a_f[chip, :, core] = a_bf.astype(F32).reshape(tj, ti, hid)
    b_f[chip] = b_bf.astype(F32)

    for load in loads[6:]:
        load.wait()
    gate = jax.nn.sigmoid(dot(x_bf, wg_ref[...]) + bg_ref[...])
    grad_out = reorder(cot_ref)
    go_out[...] = (grad_out * gate).astype(BF16).reshape(2, half, hid)
    send_go = remote(go_out.at[1 - core], go_in, c_ss.at[0], c_rs.at[0], partner, col)
    send_go.start()
    dm_f[:, core] = dot_t(go_out[core], wo_ref[...]).reshape(ti, ti, hid)

    def send_tri(block):
        return remote(
            tri_out.at[block], tri_in.at[col], t_ss.at[block], t_rs.at[col], row, block
        )

    def forward(block):
        sums = []
        a_k = [[a_f[chip, k, part] for part in range(2)] for k in range(tj)]
        for jj in range(ti):
            total = [None, None]
            for k in range(tj):
                b_row = b_f[block, k * ti + jj : k * ti + jj + 1, :]
                for part in range(2):
                    term = a_k[k][part] * b_row
                    total[part] = term if k == 0 else total[part] + term
            sums += total
        whole = jnp.concatenate(sums, 0)

        @pl.when(block == col)
        def _():
            tri_own[...] = whole

        @pl.when(block != col)
        def _():
            tri_out[block] = whole.astype(BF16)
            send_tri(block).start()

    @pl.when(core == 0)
    def _():
        pl.semaphore_wait(barrier, 2 * n_col - 1)
        pl.semaphore_signal(ready, inc=1, device_id=(partner, col), device_id_type=MESH)

    @pl.when(core == 1)
    def _():
        pl.semaphore_wait(ready, 1)

    got_a(chip, 1 - core).wait_recv()
    a_f[chip, :, 1 - core] = a_in[chip, 1 - core].astype(F32).reshape(tj, ti, hid)
    forward(chip)

    def forward_step(step, carry):
        block = jnp.where(step <= chip, step - 1, step)
        remote(
            b_out, b_in.at[block], b_ss.at[0], b_rs.at[block], 2 * block + core, col
        ).wait_recv()
        b_f[block] = b_in[block].astype(F32)
        forward(block)
        return carry

    lax.fori_loop(1, chips, forward_step, 0)

    send_go.wait_recv()
    dm_f[:, 1 - core] = dot_t(go_in[...], wo_ref[...]).reshape(ti, ti, hid)
    scaled = dm_f[...].reshape(tok, hid) * gmid_ref[...]
    scaled = scaled - jnp.mean(scaled, -1, keepdims=True)

    for step in range(1, chips):
        source_chip = source(chip, step, chips)
        got_a(source_chip, core).wait_recv()
        relay_a(step).start()
        a_f[source_chip, :, core] = a_in[source_chip, core].astype(F32).reshape(tj, ti, hid)

    triangle = tri_own[...]
    for step in range(1, n_col):
        other = source(col, step, n_col)
        remote(
            tri_out.at[0], tri_in.at[other], t_ss.at[0], t_rs.at[other], row, other
        ).wait_recv()
        triangle = triangle + tri_in[other].astype(F32)
    centred = triangle - jnp.mean(triangle, -1, keepdims=True)
    variance = jnp.mean(centred * centred, -1, keepdims=True)
    slope = jnp.mean(scaled * centred, -1, keepdims=True)
    rstd_mid = lax.rsqrt(variance + 1e-05)
    hat_mid = centred * rstd_mid
    d_tri = (rstd_mid * (scaled - hat_mid * (rstd_mid * slope))).astype(BF16)
    d_out_s[...] = d_tri

    dz_in[col] = d_tri

    def send_z(block):
        return remote(d_out_s, dz_in.at[col], z_ss.at[block], z_rs.at[col], row, block)

    def send_n(block):
        return remote(
            d_out_s, dn_in.at[chip], n_ss.at[block], n_rs.at[chip], 2 * col + core, block
        )

    for block in range(n_col):
        @pl.when(block != col)
        def _():
            send_z(block).start()

        @pl.when(chip != col)
        def _():
            send_n(block).start()

    mid_bf = (hat_mid * gmid_ref[...] + bmid_ref[...]).astype(BF16)
    ol_f[...] = (dot(mid_bf, wo_ref[...]) + bo_ref[...]).reshape(ti, 2, ti, hid)
    ol_out[...] = ol_f[:, 1 - core].reshape(half, hid)
    send_ol = remote(ol_out, ol_all.at[core], c_ss.at[1], c_rs.at[1], partner, col)
    send_ol.start()
    ol_all[core] = ol_f[:, core].reshape(half, hid)

    def backward_a(block, d_block, sums):
        out = list(sums)
        for jj in range(ti):
            d_j = [d_block[(2 * jj + part) * ti : (2 * jj + part + 1) * ti] for part in range(2)]
            for k in range(tj):
                b_row = b_f[block, k * ti + jj : k * ti + jj + 1, :]
                for part in range(2):
                    out[2 * k + part] = out[2 * k + part] + d_j[part] * b_row
        return tuple(out)

    zero = tuple(jnp.zeros((ti, hid), F32) for _ in range(2 * tj))
    sums_a = backward_a(col, d_tri.astype(F32), zero)

    for step in range(1, chips):
        source_chip = source(chip, step, chips)
        got_a(source_chip, 1 - core).wait_recv()
        a_f[source_chip, :, 1 - core] = a_in[source_chip, 1 - core].astype(F32).reshape(tj, ti, hid)

    send_ol.wait_recv()
    out_lin = ol_all[...].reshape(tok, hid)
    update = gate * out_lin
    for k in range(tj):
        stage[pl.ds(k, ti, stride=tj), :] = update[k * ti : (k + 1) * ti, :]
    upd_ref[...] = stage[...].astype(BF16).reshape(ti, tj, hid)
    d_gpre = (grad_out * out_lin * gate * (1.0 - gate)).astype(BF16)
    d_x = dot_t(d_gpre, wg_ref[...])
    slope_a, gate_a = mask * val_a * sig_a * (1.0 - sig_a), mask * sig_a
    slope_b, gate_b = mask * val_b * sig_b * (1.0 - sig_b), mask * sig_b

    send_go.wait_send()
    for step in range(chips):
        send_a(step).wait_send()
    for step in range(1, chips):
        send_b(flip(chip, step, chips)).wait_send()
        relay_a(step).wait_send()
    for block in range(n_col):
        @pl.when(block != col)
        def _():
            send_tri(block).wait_send()

    def backward_step(step, sums):
        other = source(col, step, n_col)
        remote(
            d_out_s, dz_in.at[other], z_ss.at[0], z_rs.at[other], row, other
        ).wait_recv()
        return backward_a(other, dz_in[other].astype(F32), sums)

    sums_a = lax.fori_loop(1, n_col, backward_step, sums_a)
    da_f[...] = jnp.concatenate(sums_a, 0).reshape(tj, 2, ti, hid)
    da_out[...] = da_f[:, 1 - core].reshape(tok, hid)
    send_da = remote(da_out, da_in, c_ss.at[2], c_rs.at[2], partner, col)
    send_da.start()

    def backward_b(block, d_block, sums):
        d_f[...] = d_block.astype(F32)
        out = list(sums)
        for part in range(2):
            for i in range(ti):
                d_i = d_f[pl.ds(part * ti + i, ti, stride=2 * ti), :]
                for k in range(tj):
                    out[k] = out[k] + d_i * a_f[block, k, part, i : i + 1, :]
        return tuple(out)

    def backward_b_step(step, sums):
        block = source(chip, step, chips)
        remote(
            d_out_s, dn_in.at[block], n_ss.at[0], n_rs.at[block], 2 * block + core, chip
        ).wait_recv()
        return backward_b(block, dn_in[block], sums)

    zero = tuple(jnp.zeros((ti, hid), F32) for _ in range(tj))
    sums_b = backward_b(chip, dz_in[chip], zero)
    sums_b = lax.fori_loop(1, chips, backward_b_step, sums_b)
    grad_b = jnp.concatenate(sums_b, 0)

    send_da.wait_recv()
    grad_a = da_f[:, core].reshape(tok, hid) + da_in[...]
    d_ga = (grad_a * slope_a).astype(BF16)
    d_va = (grad_a * gate_a).astype(BF16)
    d_x = d_x + dot_t(d_ga, wp_ref[:, :hid]) + dot_t(d_va, wp_ref[:, hid : 2 * hid])

    d_gb = (grad_b * slope_b).astype(BF16)
    d_vb = (grad_b * gate_b).astype(BF16)
    d_x = d_x + dot_t(d_gb, wp_ref[:, 2 * hid : 3 * hid]) + dot_t(d_vb, wp_ref[:, 3 * hid :])
    pair_grad = norm_back(d_x, hat_in, rstd_in, gin_ref[...])
    for k in range(tj):
        grad_ref[pl.ds(k, ti, stride=tj), :] = pair_grad[k * ti : (k + 1) * ti, :]

    send_ol.wait_send()
    send_da.wait_send()
    for block in range(n_col):
        @pl.when(block != col)
        def _():
            send_z(block).wait_send()

        @pl.when(chip != col)
        def _():
            send_n(block).wait_send()


def store(upd_ref, grad_ref, upd_hbm, grad_hbm, sem):
    first = pltpu.make_async_copy(upd_ref, upd_hbm, sem.at[0])
    second = pltpu.make_async_copy(grad_ref, grad_hbm, sem.at[1])
    second.start()
    first.start()
    second.wait()
    first.wait()


def per_device(n_row, n_col, pair, pair_mask, gin, bin_, wp, bp, wg, bg, gmid, bmid, wo, bo, cot):
    ti, tj, chan = pair.shape
    hid = chan
    tok, half, chips = ti * tj, ti * ti, n_row // 2
    assert tj == 2 * ti and n_row == 2 * n_col
    vec = lambda v: v.reshape(1, -1)
    dma = pltpu.SemaphoreType.DMA
    vmem = pl.BlockSpec(memory_space=pltpu.VMEM)
    operands = (pair, pair_mask, vec(gin), vec(bin_), wp, vec(bp), wg, vec(bg), vec(gmid), vec(bmid), wo, vec(bo), cot)
    update, grad = pl.pallas_call(
        functools.partial(kernel, n_row, n_col, ti, tj),
        name="triangle_step",
        out_shape=(
            jax.ShapeDtypeStruct(pair.shape, BF16),
            jax.ShapeDtypeStruct((tok, hid), F32),
        ),
        in_specs=[pl.BlockSpec(memory_space=pltpu.HBM)] * 13,
        out_specs=(vmem, vmem),
        scratch_shapes=[pltpu.VMEM(v.shape, v.dtype) for v in operands]
        + [dma((len(operands),))]
        + [
            pltpu.VMEM((tok, hid), F32),
            pltpu.VMEM((tok, hid), BF16),
            pltpu.VMEM((chips, 2, tok, hid), BF16),
            pltpu.VMEM((chips, tj, 2, ti, hid), F32),
            pltpu.VMEM((tok, hid), BF16),
            pltpu.VMEM((chips, tok, hid), BF16),
            pltpu.VMEM((chips, tok, hid), F32),
            pltpu.VMEM((tok, hid), F32),
            pltpu.VMEM((n_col, tok, hid), BF16),
            pltpu.VMEM((n_col, tok, hid), BF16),
            pltpu.VMEM((2, half, hid), BF16),
            pltpu.VMEM((half, hid), BF16),
            pltpu.VMEM((ti, 2, ti, hid), F32),
            pltpu.VMEM((tok, hid), BF16),
            pltpu.VMEM((n_col, tok, hid), BF16),
            pltpu.VMEM((chips, tok, hid), BF16),
            pltpu.VMEM((tok, hid), F32),
            pltpu.VMEM((ti, 2, ti, hid), F32),
            pltpu.VMEM((half, hid), F32),
            pltpu.VMEM((2, half, hid), F32),
            pltpu.VMEM((tj, 2, ti, hid), F32),
            pltpu.VMEM((tok, hid), F32),
            pltpu.VMEM((tok, hid), F32),
            dma((chips,)),
            dma((chips, 2)),
            dma((chips,)),
            dma((chips,)),
            dma((chips,)),
            dma((n_col,)),
            dma((n_col,)),
            dma((n_col,)),
            dma((n_col,)),
            dma((n_col,)),
            dma((chips,)),
            dma((3,)),
            dma((3,)),
            pltpu.SemaphoreType.REGULAR,
        ],
        compiler_params=pltpu.CompilerParams(
            collective_id=0, has_side_effects=True, vmem_limit_bytes=40 << 20
        ),
    )(*[pltpu.with_memory_space_constraint(v, pltpu.HBM) for v in operands])
    hbm = pl.BlockSpec(memory_space=pltpu.HBM)
    update, grad = pl.pallas_call(
        store,
        name="store_outputs",
        out_shape=(
            jax.ShapeDtypeStruct(pair.shape, BF16),
            jax.ShapeDtypeStruct((tok, hid), F32),
        ),
        in_specs=[vmem, vmem],
        out_specs=(hbm, hbm),
        scratch_shapes=[dma((2,))],
        compiler_params=pltpu.CompilerParams(vmem_limit_bytes=1 << 20),
    )(update, grad)
    return update, grad.reshape(ti, tj, hid)


def solution(mesh):
    grid = P("row", "col", None)
    placed = (grid, P("row", "col")) + (P(),) * 10 + (grid,)
    return jax.shard_map(
        functools.partial(per_device, mesh.shape["row"], mesh.shape["col"]),
        mesh=mesh,
        in_specs=placed,
        out_specs=(grid, grid),
        check_vma=False,
    )
```

```python
import functools

import jax
import jax.numpy as jnp
from jax import lax
from jax.experimental import pallas as pl
from jax.experimental.pallas import tpu as pltpu
from jax.sharding import PartitionSpec as P

F32 = jnp.float32
BF16 = jnp.bfloat16
MESH = pl.DeviceIdType.MESH


def flip(index, step, size):
    if size & (size - 1):
        return lax.rem(index + step, size)
    partner, weight = 0, 1
    while weight < size:
        mine, other = (index // weight) % 2, (step // weight) % 2
        partner = partner + weight * ((mine + other) % 2)
        weight *= 2
    return partner


def source(index, step, size):
    if size & (size - 1):
        return lax.rem(index + size - step, size)
    return flip(index, step, size)


def normalize(values):
    centred = values - jnp.mean(values, -1, keepdims=True)
    inv_std = lax.rsqrt(jnp.mean(centred * centred, -1, keepdims=True) + 1e-05)
    return centred * inv_std, inv_std


def norm_back(upstream, hat, inv_std, gain):
    scaled = upstream * gain
    return inv_std * (
        scaled
        - jnp.mean(scaled, -1, keepdims=True)
        - hat * jnp.mean(scaled * hat, -1, keepdims=True)
    )


def dot(lhs, rhs):
    return jnp.dot(lhs, rhs, preferred_element_type=F32)


def dot_t(lhs, rhs):
    return lax.dot_general(lhs, rhs, (((1,), (1,)), ((), ())), preferred_element_type=F32)


def kernel(
    n_row, n_col, ti, tj,
    pair_hbm, mask_hbm, gin_hbm, bin_hbm, wp_hbm, bp_hbm, wg_hbm, bg_hbm,
    gmid_hbm, bmid_hbm, wo_hbm, bo_hbm, cot_hbm,
    upd_ref, grad_ref,
    pair_ref, mask_ref, gin_ref, bin_ref, wp_ref, bp_ref, wg_ref, bg_ref,
    gmid_ref, bmid_ref, wo_ref, bo_ref, cot_ref, in_sem,
    stage, a_out, a_in, a_f, b_out, b_in, b_f, tri_own, tri_out, tri_in,
    go_out, go_in, dm_f, d_out_s, dz_in, dn_in, d_f, ol_f, ol_out, ol_all, da_f, da_out, da_in,
    a_ss, a_rs, af_ss, b_ss, b_rs, t_ss, t_rs, z_ss, z_rs, n_ss, n_rs, c_ss, c_rs, ready,
):
    row, col = lax.axis_index("row"), lax.axis_index("col")
    chip, core = row // 2, row % 2
    partner = row + 1 - 2 * core
    tok = ti * tj
    half = ti * ti
    chips = n_row // 2
    hid = a_out.shape[-1]

    operands = (
        (pair_hbm, pair_ref), (wp_hbm, wp_ref), (gin_hbm, gin_ref), (bin_hbm, bin_ref),
        (bp_hbm, bp_ref), (mask_hbm, mask_ref), (wg_hbm, wg_ref), (bg_hbm, bg_ref),
        (cot_hbm, cot_ref), (wo_hbm, wo_ref), (gmid_hbm, gmid_ref), (bmid_hbm, bmid_ref),
        (bo_hbm, bo_ref),
    )
    loads = [
        pltpu.make_async_copy(src, dst, in_sem.at[n]) for n, (src, dst) in enumerate(operands)
    ]
    loads[0].start()
    barrier = pltpu.get_barrier_semaphore()

    def announce(to_row, to_col):
        pl.semaphore_signal(barrier, inc=1, device_id=(to_row, to_col), device_id_type=MESH)

    for step in reversed(range(1, chips)):
        announce(2 * flip(chip, step, chips) + 1, col)
    for step in reversed(range(1, n_col)):
        announce(2 * chip, flip(col, step, n_col))
    announce(partner, col)
    for load in loads[1:]:
        load.start()

    def remote(src, dst, send, recv, to_row, to_col):
        return pltpu.make_async_remote_copy(
            src, dst, send, recv, device_id=(to_row, to_col), device_id_type=MESH
        )

    def reorder(ref):
        stage[...] = ref[...].astype(F32).reshape(tok, hid)
        return jnp.concatenate([stage[pl.ds(k, ti, stride=tj), :] for k in range(tj)], 0)

    loads[0].wait()
    hat_in, rstd_in = normalize(reorder(pair_ref))
    for load in loads[1:6]:
        load.wait()
    x_bf = (hat_in * gin_ref[...] + bin_ref[...]).astype(BF16)
    proj_b = dot(x_bf, wp_ref[:, 2 * hid :]) + bp_ref[:, 2 * hid :]
    mask_v = mask_ref[...].astype(F32)
    mask = jnp.concatenate(
        [jnp.broadcast_to(mask_v[:, k : k + 1], (ti, hid)) for k in range(tj)], 0
    )
    sig_b = jax.nn.sigmoid(proj_b[:, :hid])
    val_b = proj_b[:, hid:]
    b_bf = (mask * sig_b * val_b).astype(BF16)
    b_out[...] = b_bf

    @pl.when(core == 1)
    def _():
        pl.semaphore_wait(barrier, 2 * chips - 1)
        pl.semaphore_signal(ready, inc=1, device_id=(partner, col), device_id_type=MESH)

    @pl.when(core == 0)
    def _():
        pl.semaphore_wait(ready, 1)


    def send_b(to):
        return remote(b_out, b_in.at[chip], b_ss.at[to], b_rs.at[chip], 2 * to + core, col)

    for to in range(chips):
        @pl.when(to != chip)
        def _():
            send_b(to).start()

    proj_a = dot(x_bf, wp_ref[:, : 2 * hid]) + bp_ref[:, : 2 * hid]
    sig_a = jax.nn.sigmoid(proj_a[:, :hid])
    val_a = proj_a[:, hid:]
    a_bf = (mask * sig_a * val_a).astype(BF16)
    a_out[...] = a_bf

    def send_a(step):
        to = 2 * flip(chip, step, chips) + core if step else partner
        return remote(a_out, a_in.at[chip, core], a_ss.at[step], a_rs.at[chip, core], to, col)

    def relay_a(step):
        source_chip = source(chip, step, chips)
        held = a_in.at[source_chip, core]
        return remote(held, held, af_ss.at[source_chip], a_rs.at[source_chip, core], partner, col)

    def got_a(source_chip, source_core):
        return remote(
            a_out, a_in.at[source_chip, source_core], a_ss.at[0],
            a_rs.at[source_chip, source_core], partner, col,
        )

    for step in range(chips):
        send_a(step).start()
    a_f[chip, :, core] = a_bf.astype(F32).reshape(tj, ti, hid)
    b_f[chip] = b_bf.astype(F32)

    for load in loads[6:]:
        load.wait()
    gate = jax.nn.sigmoid(dot(x_bf, wg_ref[...]) + bg_ref[...])
    grad_out = reorder(cot_ref)
    go_out[...] = (grad_out * gate).astype(BF16).reshape(2, half, hid)
    send_go = remote(go_out.at[1 - core], go_in, c_ss.at[0], c_rs.at[0], partner, col)
    send_go.start()
    dm_f[:, core] = dot_t(go_out[core], wo_ref[...]).reshape(ti, ti, hid)

    def send_tri(block):
        return remote(
            tri_out.at[block], tri_in.at[col], t_ss.at[block], t_rs.at[col], row, block
        )

    def forward(block):
        sums = []
        a_k = [[a_f[chip, k, part] for part in range(2)] for k in range(tj)]
        for jj in range(ti):
            total = [None, None]
            for k in range(tj):
                b_row = b_f[block, k * ti + jj : k * ti + jj + 1, :]
                for part in range(2):
                    term = a_k[k][part] * b_row
                    total[part] = term if k == 0 else total[part] + term
            sums += total
        whole = jnp.concatenate(sums, 0)

        @pl.when(block == col)
        def _():
            tri_own[...] = whole

        @pl.when(block != col)
        def _():
            tri_out[block] = whole.astype(BF16)
            send_tri(block).start()

    @pl.when(core == 0)
    def _():
        pl.semaphore_wait(barrier, 2 * n_col - 1)
        pl.semaphore_signal(ready, inc=1, device_id=(partner, col), device_id_type=MESH)

    @pl.when(core == 1)
    def _():
        pl.semaphore_wait(ready, 1)

    got_a(chip, 1 - core).wait_recv()
    a_f[chip, :, 1 - core] = a_in[chip, 1 - core].astype(F32).reshape(tj, ti, hid)
    forward(chip)

    def forward_step(step, carry):
        block = jnp.where(step <= chip, step - 1, step)
        remote(
            b_out, b_in.at[block], b_ss.at[0], b_rs.at[block], 2 * block + core, col
        ).wait_recv()
        b_f[block] = b_in[block].astype(F32)
        forward(block)
        return carry

    lax.fori_loop(1, chips, forward_step, 0)

    send_go.wait_recv()
    dm_f[:, 1 - core] = dot_t(go_in[...], wo_ref[...]).reshape(ti, ti, hid)
    scaled = dm_f[...].reshape(tok, hid) * gmid_ref[...]
    scaled = scaled - jnp.mean(scaled, -1, keepdims=True)

    for step in range(1, chips):
        source_chip = source(chip, step, chips)
        got_a(source_chip, core).wait_recv()
        relay_a(step).start()
        a_f[source_chip, :, core] = a_in[source_chip, core].astype(F32).reshape(tj, ti, hid)

    triangle = tri_own[...]
    for step in range(1, n_col):
        other = source(col, step, n_col)
        remote(
            tri_out.at[0], tri_in.at[other], t_ss.at[0], t_rs.at[other], row, other
        ).wait_recv()
        triangle = triangle + tri_in[other].astype(F32)
    centred = triangle - jnp.mean(triangle, -1, keepdims=True)
    variance = jnp.mean(centred * centred, -1, keepdims=True)
    slope = jnp.mean(scaled * centred, -1, keepdims=True)
    rstd_mid = lax.rsqrt(variance + 1e-05)
    hat_mid = centred * rstd_mid
    d_tri = (rstd_mid * (scaled - hat_mid * (rstd_mid * slope))).astype(BF16)
    d_out_s[...] = d_tri

    dz_in[col] = d_tri

    def send_z(block):
        return remote(d_out_s, dz_in.at[col], z_ss.at[block], z_rs.at[col], row, block)

    def send_n(block):
        return remote(
            d_out_s, dn_in.at[chip], n_ss.at[block], n_rs.at[chip], 2 * col + core, block
        )

    for block in range(n_col):
        @pl.when(block != col)
        def _():
            send_z(block).start()

        @pl.when(chip != col)
        def _():
            send_n(block).start()

    mid_bf = (hat_mid * gmid_ref[...] + bmid_ref[...]).astype(BF16)
    ol_f[...] = (dot(mid_bf, wo_ref[...]) + bo_ref[...]).reshape(ti, 2, ti, hid)
    ol_out[...] = ol_f[:, 1 - core].reshape(half, hid)
    send_ol = remote(ol_out, ol_all.at[core], c_ss.at[1], c_rs.at[1], partner, col)
    send_ol.start()
    ol_all[core] = ol_f[:, core].reshape(half, hid)

    def backward_a(block, d_block, sums):
        out = list(sums)
        for jj in range(ti):
            d_j = [d_block[(2 * jj + part) * ti : (2 * jj + part + 1) * ti] for part in range(2)]
            for k in range(tj):
                b_row = b_f[block, k * ti + jj : k * ti + jj + 1, :]
                for part in range(2):
                    out[2 * k + part] = out[2 * k + part] + d_j[part] * b_row
        return tuple(out)

    zero = tuple(jnp.zeros((ti, hid), F32) for _ in range(2 * tj))
    sums_a = backward_a(col, d_tri.astype(F32), zero)

    for step in range(1, chips):
        source_chip = source(chip, step, chips)
        got_a(source_chip, 1 - core).wait_recv()
        a_f[source_chip, :, 1 - core] = a_in[source_chip, 1 - core].astype(F32).reshape(tj, ti, hid)

    send_ol.wait_recv()
    out_lin = ol_all[...].reshape(tok, hid)
    update = gate * out_lin
    for k in range(tj):
        stage[pl.ds(k, ti, stride=tj), :] = update[k * ti : (k + 1) * ti, :]
    upd_ref[...] = stage[...].astype(BF16).reshape(ti, tj, hid)
    d_gpre = (grad_out * out_lin * gate * (1.0 - gate)).astype(BF16)
    d_x = dot_t(d_gpre, wg_ref[...])
    slope_a, gate_a = mask * val_a * sig_a * (1.0 - sig_a), mask * sig_a
    slope_b, gate_b = mask * val_b * sig_b * (1.0 - sig_b), mask * sig_b

    send_go.wait_send()
    for step in range(chips):
        send_a(step).wait_send()
    for step in range(1, chips):
        send_b(flip(chip, step, chips)).wait_send()
        relay_a(step).wait_send()
    for block in range(n_col):
        @pl.when(block != col)
        def _():
            send_tri(block).wait_send()

    def backward_step(step, sums):
        other = source(col, step, n_col)
        remote(
            d_out_s, dz_in.at[other], z_ss.at[0], z_rs.at[other], row, other
        ).wait_recv()
        return backward_a(other, dz_in[other].astype(F32), sums)

    sums_a = lax.fori_loop(1, n_col, backward_step, sums_a)
    da_f[...] = jnp.concatenate(sums_a, 0).reshape(tj, 2, ti, hid)
    da_out[...] = da_f[:, 1 - core].reshape(tok, hid)
    send_da = remote(da_out, da_in, c_ss.at[2], c_rs.at[2], partner, col)
    send_da.start()

    def backward_b(block, d_block, sums):
        d_f[...] = d_block.astype(F32)
        out = list(sums)
        for part in range(2):
            for i in range(ti):
                d_i = d_f[pl.ds(part * ti + i, ti, stride=2 * ti), :]
                for k in range(tj):
                    out[k] = out[k] + d_i * a_f[block, k, part, i : i + 1, :]
        return tuple(out)

    def backward_b_step(step, sums):
        block = source(chip, step, chips)
        remote(
            d_out_s, dn_in.at[block], n_ss.at[0], n_rs.at[block], 2 * block + core, chip
        ).wait_recv()
        return backward_b(block, dn_in[block], sums)

    zero = tuple(jnp.zeros((ti, hid), F32) for _ in range(tj))
    sums_b = backward_b(chip, dz_in[chip], zero)
    sums_b = lax.fori_loop(1, chips - 1, backward_b_step, sums_b)

    send_da.wait_recv()
    grad_a = da_f[:, core].reshape(tok, hid) + da_in[...]
    d_ga = (grad_a * slope_a).astype(BF16)
    d_va = (grad_a * gate_a).astype(BF16)
    d_x = d_x + dot_t(d_ga, wp_ref[:, :hid]) + dot_t(d_va, wp_ref[:, hid : 2 * hid])

    sums_b = backward_b_step(chips - 1, sums_b)
    grad_b = jnp.concatenate(sums_b, 0)

    d_gb = (grad_b * slope_b).astype(BF16)
    d_vb = (grad_b * gate_b).astype(BF16)
    d_x = d_x + dot_t(d_gb, wp_ref[:, 2 * hid : 3 * hid]) + dot_t(d_vb, wp_ref[:, 3 * hid :])
    pair_grad = norm_back(d_x, hat_in, rstd_in, gin_ref[...])
    for k in range(tj):
        grad_ref[pl.ds(k, ti, stride=tj), :] = pair_grad[k * ti : (k + 1) * ti, :]

    send_ol.wait_send()
    send_da.wait_send()
    for block in range(n_col):
        @pl.when(block != col)
        def _():
            send_z(block).wait_send()

        @pl.when(chip != col)
        def _():
            send_n(block).wait_send()


def store(upd_ref, grad_ref, upd_hbm, grad_hbm, sem):
    first = pltpu.make_async_copy(upd_ref, upd_hbm, sem.at[0])
    second = pltpu.make_async_copy(grad_ref, grad_hbm, sem.at[1])
    second.start()
    first.start()
    second.wait()
    first.wait()


def per_device(n_row, n_col, pair, pair_mask, gin, bin_, wp, bp, wg, bg, gmid, bmid, wo, bo, cot):
    ti, tj, chan = pair.shape
    hid = chan
    tok, half, chips = ti * tj, ti * ti, n_row // 2
    assert tj == 2 * ti and n_row == 2 * n_col
    vec = lambda v: v.reshape(1, -1)
    dma = pltpu.SemaphoreType.DMA
    vmem = pl.BlockSpec(memory_space=pltpu.VMEM)
    operands = (pair, pair_mask, vec(gin), vec(bin_), wp, vec(bp), wg, vec(bg), vec(gmid), vec(bmid), wo, vec(bo), cot)
    update, grad = pl.pallas_call(
        functools.partial(kernel, n_row, n_col, ti, tj),
        name="triangle_step",
        out_shape=(
            jax.ShapeDtypeStruct(pair.shape, BF16),
            jax.ShapeDtypeStruct((tok, hid), F32),
        ),
        in_specs=[pl.BlockSpec(memory_space=pltpu.HBM)] * 13,
        out_specs=(vmem, vmem),
        scratch_shapes=[pltpu.VMEM(v.shape, v.dtype) for v in operands]
        + [dma((len(operands),))]
        + [
            pltpu.VMEM((tok, hid), F32),
            pltpu.VMEM((tok, hid), BF16),
            pltpu.VMEM((chips, 2, tok, hid), BF16),
            pltpu.VMEM((chips, tj, 2, ti, hid), F32),
            pltpu.VMEM((tok, hid), BF16),
            pltpu.VMEM((chips, tok, hid), BF16),
            pltpu.VMEM((chips, tok, hid), F32),
            pltpu.VMEM((tok, hid), F32),
            pltpu.VMEM((n_col, tok, hid), BF16),
            pltpu.VMEM((n_col, tok, hid), BF16),
            pltpu.VMEM((2, half, hid), BF16),
            pltpu.VMEM((half, hid), BF16),
            pltpu.VMEM((ti, 2, ti, hid), F32),
            pltpu.VMEM((tok, hid), BF16),
            pltpu.VMEM((n_col, tok, hid), BF16),
            pltpu.VMEM((chips, tok, hid), BF16),
            pltpu.VMEM((tok, hid), F32),
            pltpu.VMEM((ti, 2, ti, hid), F32),
            pltpu.VMEM((half, hid), F32),
            pltpu.VMEM((2, half, hid), F32),
            pltpu.VMEM((tj, 2, ti, hid), F32),
            pltpu.VMEM((tok, hid), F32),
            pltpu.VMEM((tok, hid), F32),
            dma((chips,)),
            dma((chips, 2)),
            dma((chips,)),
            dma((chips,)),
            dma((chips,)),
            dma((n_col,)),
            dma((n_col,)),
            dma((n_col,)),
            dma((n_col,)),
            dma((n_col,)),
            dma((chips,)),
            dma((3,)),
            dma((3,)),
            pltpu.SemaphoreType.REGULAR,
        ],
        compiler_params=pltpu.CompilerParams(
            collective_id=0, has_side_effects=True, vmem_limit_bytes=40 << 20
        ),
    )(*[pltpu.with_memory_space_constraint(v, pltpu.HBM) for v in operands])
    hbm = pl.BlockSpec(memory_space=pltpu.HBM)
    update, grad = pl.pallas_call(
        store,
        name="store_outputs",
        out_shape=(
            jax.ShapeDtypeStruct(pair.shape, BF16),
            jax.ShapeDtypeStruct((tok, hid), F32),
        ),
        in_specs=[vmem, vmem],
        out_specs=(hbm, hbm),
        scratch_shapes=[dma((2,))],
        compiler_params=pltpu.CompilerParams(vmem_limit_bytes=1 << 20),
    )(update, grad)
    return update, grad.reshape(ti, tj, hid)


def solution(mesh):
    grid = P("row", "col", None)
    placed = (grid, P("row", "col")) + (P(),) * 10 + (grid,)
    return jax.shard_map(
        functools.partial(per_device, mesh.shape["row"], mesh.shape["col"]),
        mesh=mesh,
        in_specs=placed,
        out_specs=(grid, grid),
        check_vma=False,
    )
```

```python
import functools

import jax
import jax.numpy as jnp
from jax import lax
from jax.experimental import pallas as pl
from jax.experimental.pallas import tpu as pltpu
from jax.sharding import PartitionSpec as P

F32 = jnp.float32
BF16 = jnp.bfloat16
MESH = pl.DeviceIdType.MESH


def flip(index, step, size):
    if size & (size - 1):
        return lax.rem(index + step, size)
    partner, weight = 0, 1
    while weight < size:
        mine, other = (index // weight) % 2, (step // weight) % 2
        partner = partner + weight * ((mine + other) % 2)
        weight *= 2
    return partner


def source(index, step, size):
    if size & (size - 1):
        return lax.rem(index + size - step, size)
    return flip(index, step, size)


def normalize(values):
    centred = values - jnp.mean(values, -1, keepdims=True)
    inv_std = lax.rsqrt(jnp.mean(centred * centred, -1, keepdims=True) + 1e-05)
    return centred * inv_std, inv_std


def norm_back(upstream, hat, inv_std, gain):
    scaled = upstream * gain
    return inv_std * (
        scaled
        - jnp.mean(scaled, -1, keepdims=True)
        - hat * jnp.mean(scaled * hat, -1, keepdims=True)
    )


def dot(lhs, rhs):
    return jnp.dot(lhs, rhs, preferred_element_type=F32)


def dot_t(lhs, rhs):
    return lax.dot_general(lhs, rhs, (((1,), (1,)), ((), ())), preferred_element_type=F32)


def kernel(
    n_row, n_col, ti, tj,
    pair_hbm, mask_hbm, gin_hbm, bin_hbm, wp_hbm, bp_hbm, wg_hbm, bg_hbm,
    gmid_hbm, bmid_hbm, wo_hbm, bo_hbm, cot_hbm,
    upd_ref, grad_ref,
    pair_ref, mask_ref, gin_ref, bin_ref, wp_ref, bp_ref, wg_ref, bg_ref,
    gmid_ref, bmid_ref, wo_ref, bo_ref, cot_ref, in_sem,
    stage, a_out, a_in, a_f, b_out, b_in, b_f, tri_own, tri_out, tri_in,
    go_out, go_in, dm_f, d_out_s, dz_in, dn_in, d_f, ol_f, ol_out, ol_all, da_f, da_out, da_in,
    a_ss, a_rs, af_ss, b_ss, b_rs, t_ss, t_rs, z_ss, z_rs, n_ss, n_rs, c_ss, c_rs, ready,
):
    row, col = lax.axis_index("row"), lax.axis_index("col")
    chip, core = row // 2, row % 2
    partner = row + 1 - 2 * core
    tok = ti * tj
    half = ti * ti
    chips = n_row // 2
    hid = a_out.shape[-1]

    operands = (
        (pair_hbm, pair_ref), (wp_hbm, wp_ref), (gin_hbm, gin_ref), (bin_hbm, bin_ref),
        (bp_hbm, bp_ref), (mask_hbm, mask_ref), (wg_hbm, wg_ref), (bg_hbm, bg_ref),
        (cot_hbm, cot_ref), (wo_hbm, wo_ref), (gmid_hbm, gmid_ref), (bmid_hbm, bmid_ref),
        (bo_hbm, bo_ref),
    )
    loads = [
        pltpu.make_async_copy(src, dst, in_sem.at[n]) for n, (src, dst) in enumerate(operands)
    ]
    loads[0].start()
    barrier = pltpu.get_barrier_semaphore()

    def announce(to_row, to_col):
        pl.semaphore_signal(barrier, inc=1, device_id=(to_row, to_col), device_id_type=MESH)

    for step in reversed(range(1, chips)):
        announce(2 * flip(chip, step, chips) + core, col)
    announce(partner, col)
    for block in reversed(range(1, n_col)):
        @pl.when(block > col)
        def _():
            announce(row, block)

    for load in loads[1:]:
        load.start()

    def remote(src, dst, send, recv, to_row, to_col):
        return pltpu.make_async_remote_copy(
            src, dst, send, recv, device_id=(to_row, to_col), device_id_type=MESH
        )

    def reorder(ref):
        stage[...] = ref[...].astype(F32).reshape(tok, hid)
        return jnp.concatenate([stage[pl.ds(k, ti, stride=tj), :] for k in range(tj)], 0)

    loads[0].wait()
    hat_in, rstd_in = normalize(reorder(pair_ref))
    for load in loads[1:6]:
        load.wait()
    x_bf = (hat_in * gin_ref[...] + bin_ref[...]).astype(BF16)
    proj_b = dot(x_bf, wp_ref[:, 2 * hid :]) + bp_ref[:, 2 * hid :]
    mask_v = mask_ref[...].astype(F32)
    mask = jnp.concatenate(
        [jnp.broadcast_to(mask_v[:, k : k + 1], (ti, hid)) for k in range(tj)], 0
    )
    sig_b = jax.nn.sigmoid(proj_b[:, :hid])
    val_b = proj_b[:, hid:]
    b_bf = (mask * sig_b * val_b).astype(BF16)
    b_out[...] = b_bf

    pl.semaphore_wait(barrier, chips + col)

    def send_b(to):
        return remote(b_out, b_in.at[chip], b_ss.at[to], b_rs.at[chip], 2 * to + core, col)

    for to in range(chips):
        @pl.when(to != chip)
        def _():
            send_b(to).start()

    for block in range(n_col - 1):
        @pl.when(block < col)
        def _():
            pl.semaphore_signal(ready, inc=1, device_id=(row, block), device_id_type=MESH)

    proj_a = dot(x_bf, wp_ref[:, : 2 * hid]) + bp_ref[:, : 2 * hid]
    sig_a = jax.nn.sigmoid(proj_a[:, :hid])
    val_a = proj_a[:, hid:]
    a_bf = (mask * sig_a * val_a).astype(BF16)
    a_out[...] = a_bf

    def send_a(step):
        to = 2 * flip(chip, step, chips) + core if step else partner
        return remote(a_out, a_in.at[chip, core], a_ss.at[step], a_rs.at[chip, core], to, col)

    def relay_a(step):
        source_chip = source(chip, step, chips)
        held = a_in.at[source_chip, core]
        return remote(held, held, af_ss.at[source_chip], a_rs.at[source_chip, core], partner, col)

    def got_a(source_chip, source_core):
        return remote(
            a_out, a_in.at[source_chip, source_core], a_ss.at[0],
            a_rs.at[source_chip, source_core], partner, col,
        )

    for step in range(chips):
        send_a(step).start()
    a_f[chip, :, core] = a_bf.astype(F32).reshape(tj, ti, hid)
    b_f[chip] = b_bf.astype(F32)

    for load in loads[6:]:
        load.wait()
    gate = jax.nn.sigmoid(dot(x_bf, wg_ref[...]) + bg_ref[...])
    grad_out = reorder(cot_ref)
    go_out[...] = (grad_out * gate).astype(BF16).reshape(2, half, hid)
    send_go = remote(go_out.at[1 - core], go_in, c_ss.at[0], c_rs.at[0], partner, col)
    send_go.start()
    dm_f[:, core] = dot_t(go_out[core], wo_ref[...]).reshape(ti, ti, hid)

    def send_tri(block):
        return remote(
            tri_out.at[block], tri_in.at[col], t_ss.at[block], t_rs.at[col], row, block
        )

    def forward(block):
        sums = []
        a_k = [[a_f[chip, k, part] for part in range(2)] for k in range(tj)]
        for jj in range(ti):
            total = [None, None]
            for k in range(tj):
                b_row = b_f[block, k * ti + jj : k * ti + jj + 1, :]
                for part in range(2):
                    term = a_k[k][part] * b_row
                    total[part] = term if k == 0 else total[part] + term
            sums += total
        whole = jnp.concatenate(sums, 0)

        @pl.when(block == col)
        def _():
            tri_own[...] = whole

        @pl.when(block != col)
        def _():
            tri_out[block] = whole.astype(BF16)
            send_tri(block).start()

    @pl.when(col < n_col - 1)
    def _():
        pl.semaphore_wait(ready, n_col - 1 - col)

    got_a(chip, 1 - core).wait_recv()
    a_f[chip, :, 1 - core] = a_in[chip, 1 - core].astype(F32).reshape(tj, ti, hid)
    forward(chip)

    def forward_step(step, carry):
        block = jnp.where(step <= chip, step - 1, step)
        remote(
            b_out, b_in.at[block], b_ss.at[0], b_rs.at[block], 2 * block + core, col
        ).wait_recv()
        b_f[block] = b_in[block].astype(F32)
        forward(block)
        return carry

    lax.fori_loop(1, chips, forward_step, 0)

    send_go.wait_recv()
    dm_f[:, 1 - core] = dot_t(go_in[...], wo_ref[...]).reshape(ti, ti, hid)
    scaled = dm_f[...].reshape(tok, hid) * gmid_ref[...]
    scaled = scaled - jnp.mean(scaled, -1, keepdims=True)

    for step in range(1, chips):
        source_chip = source(chip, step, chips)
        got_a(source_chip, core).wait_recv()
        relay_a(step).start()
        a_f[source_chip, :, core] = a_in[source_chip, core].astype(F32).reshape(tj, ti, hid)

    triangle = tri_own[...]
    for step in range(1, n_col):
        other = source(col, step, n_col)
        remote(
            tri_out.at[0], tri_in.at[other], t_ss.at[0], t_rs.at[other], row, other
        ).wait_recv()
        triangle = triangle + tri_in[other].astype(F32)
    centred = triangle - jnp.mean(triangle, -1, keepdims=True)
    variance = jnp.mean(centred * centred, -1, keepdims=True)
    slope = jnp.mean(scaled * centred, -1, keepdims=True)
    rstd_mid = lax.rsqrt(variance + 1e-05)
    hat_mid = centred * rstd_mid
    d_tri = (rstd_mid * (scaled - hat_mid * (rstd_mid * slope))).astype(BF16)
    d_out_s[...] = d_tri

    dz_in[col] = d_tri

    def send_z(block):
        return remote(d_out_s, dz_in.at[col], z_ss.at[block], z_rs.at[col], row, block)

    def send_n(block):
        return remote(
            d_out_s, dn_in.at[chip], n_ss.at[block], n_rs.at[chip], 2 * col + core, block
        )

    for block in range(n_col):
        @pl.when(block != col)
        def _():
            send_z(block).start()

        @pl.when(chip != col)
        def _():
            send_n(block).start()

    mid_bf = (hat_mid * gmid_ref[...] + bmid_ref[...]).astype(BF16)
    ol_f[...] = (dot(mid_bf, wo_ref[...]) + bo_ref[...]).reshape(ti, 2, ti, hid)
    ol_out[...] = ol_f[:, 1 - core].reshape(half, hid)
    send_ol = remote(ol_out, ol_all.at[core], c_ss.at[1], c_rs.at[1], partner, col)
    send_ol.start()
    ol_all[core] = ol_f[:, core].reshape(half, hid)

    def backward_a(block, d_block, sums):
        out = list(sums)
        for jj in range(ti):
            d_j = [d_block[(2 * jj + part) * ti : (2 * jj + part + 1) * ti] for part in range(2)]
            for k in range(tj):
                b_row = b_f[block, k * ti + jj : k * ti + jj + 1, :]
                for part in range(2):
                    out[2 * k + part] = out[2 * k + part] + d_j[part] * b_row
        return tuple(out)

    zero = tuple(jnp.zeros((ti, hid), F32) for _ in range(2 * tj))
    sums_a = backward_a(col, d_tri.astype(F32), zero)

    for step in range(1, chips):
        source_chip = source(chip, step, chips)
        got_a(source_chip, 1 - core).wait_recv()
        a_f[source_chip, :, 1 - core] = a_in[source_chip, 1 - core].astype(F32).reshape(tj, ti, hid)

    send_ol.wait_recv()
    out_lin = ol_all[...].reshape(tok, hid)
    update = gate * out_lin
    for k in range(tj):
        stage[pl.ds(k, ti, stride=tj), :] = update[k * ti : (k + 1) * ti, :]
    upd_ref[...] = stage[...].astype(BF16).reshape(ti, tj, hid)
    d_gpre = (grad_out * out_lin * gate * (1.0 - gate)).astype(BF16)
    d_x = dot_t(d_gpre, wg_ref[...])
    slope_a, gate_a = mask * val_a * sig_a * (1.0 - sig_a), mask * sig_a
    slope_b, gate_b = mask * val_b * sig_b * (1.0 - sig_b), mask * sig_b

    send_go.wait_send()
    for step in range(chips):
        send_a(step).wait_send()
    for step in range(1, chips):
        send_b(flip(chip, step, chips)).wait_send()
        relay_a(step).wait_send()
    for block in range(n_col):
        @pl.when(block != col)
        def _():
            send_tri(block).wait_send()

    def backward_step(step, sums):
        other = source(col, step, n_col)
        remote(
            d_out_s, dz_in.at[other], z_ss.at[0], z_rs.at[other], row, other
        ).wait_recv()
        return backward_a(other, dz_in[other].astype(F32), sums)

    sums_a = lax.fori_loop(1, n_col, backward_step, sums_a)
    da_f[...] = jnp.concatenate(sums_a, 0).reshape(tj, 2, ti, hid)
    da_out[...] = da_f[:, 1 - core].reshape(tok, hid)
    send_da = remote(da_out, da_in, c_ss.at[2], c_rs.at[2], partner, col)
    send_da.start()

    def backward_b(block, d_block, sums):
        d_f[...] = d_block.astype(F32)
        out = list(sums)
        for part in range(2):
            for i in range(ti):
                d_i = d_f[pl.ds(part * ti + i, ti, stride=2 * ti), :]
                for k in range(tj):
                    out[k] = out[k] + d_i * a_f[block, k, part, i : i + 1, :]
        return tuple(out)

    def backward_b_step(step, sums):
        block = source(chip, step, chips)
        remote(
            d_out_s, dn_in.at[block], n_ss.at[0], n_rs.at[block], 2 * block + core, chip
        ).wait_recv()
        return backward_b(block, dn_in[block], sums)

    zero = tuple(jnp.zeros((ti, hid), F32) for _ in range(tj))
    sums_b = backward_b(chip, dz_in[chip], zero)
    sums_b = lax.fori_loop(1, chips - 1, backward_b_step, sums_b)

    send_da.wait_recv()
    grad_a = da_f[:, core].reshape(tok, hid) + da_in[...]
    d_ga = (grad_a * slope_a).astype(BF16)
    d_va = (grad_a * gate_a).astype(BF16)
    d_x = d_x + dot_t(d_ga, wp_ref[:, :hid]) + dot_t(d_va, wp_ref[:, hid : 2 * hid])

    sums_b = backward_b_step(chips - 1, sums_b)
    grad_b = jnp.concatenate(sums_b, 0)

    d_gb = (grad_b * slope_b).astype(BF16)
    d_vb = (grad_b * gate_b).astype(BF16)
    d_x = d_x + dot_t(d_gb, wp_ref[:, 2 * hid : 3 * hid]) + dot_t(d_vb, wp_ref[:, 3 * hid :])
    pair_grad = norm_back(d_x, hat_in, rstd_in, gin_ref[...])
    for k in range(tj):
        grad_ref[pl.ds(k, ti, stride=tj), :] = pair_grad[k * ti : (k + 1) * ti, :]

    send_ol.wait_send()
    send_da.wait_send()
    for block in range(n_col):
        @pl.when(block != col)
        def _():
            send_z(block).wait_send()

        @pl.when(chip != col)
        def _():
            send_n(block).wait_send()


def store(upd_ref, grad_ref, upd_hbm, grad_hbm, sem):
    first = pltpu.make_async_copy(upd_ref, upd_hbm, sem.at[0])
    second = pltpu.make_async_copy(grad_ref, grad_hbm, sem.at[1])
    second.start()
    first.start()
    second.wait()
    first.wait()


def per_device(n_row, n_col, pair, pair_mask, gin, bin_, wp, bp, wg, bg, gmid, bmid, wo, bo, cot):
    ti, tj, chan = pair.shape
    hid = chan
    tok, half, chips = ti * tj, ti * ti, n_row // 2
    assert tj == 2 * ti and n_row == 2 * n_col
    vec = lambda v: v.reshape(1, -1)
    dma = pltpu.SemaphoreType.DMA
    vmem = pl.BlockSpec(memory_space=pltpu.VMEM)
    operands = (pair, pair_mask, vec(gin), vec(bin_), wp, vec(bp), wg, vec(bg), vec(gmid), vec(bmid), wo, vec(bo), cot)
    update, grad = pl.pallas_call(
        functools.partial(kernel, n_row, n_col, ti, tj),
        name="triangle_step",
        out_shape=(
            jax.ShapeDtypeStruct(pair.shape, BF16),
            jax.ShapeDtypeStruct((tok, hid), F32),
        ),
        in_specs=[pl.BlockSpec(memory_space=pltpu.HBM)] * 13,
        out_specs=(vmem, vmem),
        scratch_shapes=[pltpu.VMEM(v.shape, v.dtype) for v in operands]
        + [dma((len(operands),))]
        + [
            pltpu.VMEM((tok, hid), F32),
            pltpu.VMEM((tok, hid), BF16),
            pltpu.VMEM((chips, 2, tok, hid), BF16),
            pltpu.VMEM((chips, tj, 2, ti, hid), F32),
            pltpu.VMEM((tok, hid), BF16),
            pltpu.VMEM((chips, tok, hid), BF16),
            pltpu.VMEM((chips, tok, hid), F32),
            pltpu.VMEM((tok, hid), F32),
            pltpu.VMEM((n_col, tok, hid), BF16),
            pltpu.VMEM((n_col, tok, hid), BF16),
            pltpu.VMEM((2, half, hid), BF16),
            pltpu.VMEM((half, hid), BF16),
            pltpu.VMEM((ti, 2, ti, hid), F32),
            pltpu.VMEM((tok, hid), BF16),
            pltpu.VMEM((n_col, tok, hid), BF16),
            pltpu.VMEM((chips, tok, hid), BF16),
            pltpu.VMEM((tok, hid), F32),
            pltpu.VMEM((ti, 2, ti, hid), F32),
            pltpu.VMEM((half, hid), F32),
            pltpu.VMEM((2, half, hid), F32),
            pltpu.VMEM((tj, 2, ti, hid), F32),
            pltpu.VMEM((tok, hid), F32),
            pltpu.VMEM((tok, hid), F32),
            dma((chips,)),
            dma((chips, 2)),
            dma((chips,)),
            dma((chips,)),
            dma((chips,)),
            dma((n_col,)),
            dma((n_col,)),
            dma((n_col,)),
            dma((n_col,)),
            dma((n_col,)),
            dma((chips,)),
            dma((3,)),
            dma((3,)),
            pltpu.SemaphoreType.REGULAR,
        ],
        compiler_params=pltpu.CompilerParams(
            collective_id=0, has_side_effects=True, vmem_limit_bytes=40 << 20
        ),
    )(*[pltpu.with_memory_space_constraint(v, pltpu.HBM) for v in operands])
    hbm = pl.BlockSpec(memory_space=pltpu.HBM)
    update, grad = pl.pallas_call(
        store,
        name="store_outputs",
        out_shape=(
            jax.ShapeDtypeStruct(pair.shape, BF16),
            jax.ShapeDtypeStruct((tok, hid), F32),
        ),
        in_specs=[vmem, vmem],
        out_specs=(hbm, hbm),
        scratch_shapes=[dma((2,))],
        compiler_params=pltpu.CompilerParams(vmem_limit_bytes=1 << 20),
    )(update, grad)
    return update, grad.reshape(ti, tj, hid)


def solution(mesh):
    grid = P("row", "col", None)
    placed = (grid, P("row", "col")) + (P(),) * 10 + (grid,)
    return jax.shard_map(
        functools.partial(per_device, mesh.shape["row"], mesh.shape["col"]),
        mesh=mesh,
        in_specs=placed,
        out_specs=(grid, grid),
        check_vma=False,
    )
```

```python
import functools

import jax
import jax.numpy as jnp
from jax import lax
from jax.experimental import pallas as pl
from jax.experimental.pallas import tpu as pltpu
from jax.sharding import PartitionSpec as P

F32 = jnp.float32
BF16 = jnp.bfloat16
MESH = pl.DeviceIdType.MESH


def flip(index, step, size):
    if size & (size - 1):
        return lax.rem(index + step, size)
    partner, weight = 0, 1
    while weight < size:
        mine, other = (index // weight) % 2, (step // weight) % 2
        partner = partner + weight * ((mine + other) % 2)
        weight *= 2
    return partner


def source(index, step, size):
    if size & (size - 1):
        return lax.rem(index + size - step, size)
    return flip(index, step, size)


def normalize(values):
    centred = values - jnp.mean(values, -1, keepdims=True)
    inv_std = lax.rsqrt(jnp.mean(centred * centred, -1, keepdims=True) + 1e-05)
    return centred * inv_std, inv_std


def norm_back(upstream, hat, inv_std, gain):
    scaled = upstream * gain
    return inv_std * (
        scaled
        - jnp.mean(scaled, -1, keepdims=True)
        - hat * jnp.mean(scaled * hat, -1, keepdims=True)
    )


def dot(lhs, rhs):
    return jnp.dot(lhs, rhs, preferred_element_type=F32)


def dot_t(lhs, rhs):
    return lax.dot_general(lhs, rhs, (((1,), (1,)), ((), ())), preferred_element_type=F32)


def kernel(
    n_row, n_col, ti, tj,
    pair_hbm, mask_hbm, gin_hbm, bin_hbm, wp_hbm, bp_hbm, wg_hbm, bg_hbm,
    gmid_hbm, bmid_hbm, wo_hbm, bo_hbm, cot_hbm,
    upd_ref, grad_ref,
    pair_ref, mask_ref, gin_ref, bin_ref, wp_ref, bp_ref, wg_ref, bg_ref,
    gmid_ref, bmid_ref, wo_ref, bo_ref, cot_ref, in_sem,
    stage, a_out, a_in, a_f, b_out, b_in, b_f, tri_own, tri_out, tri_in,
    go_out, go_in, dm_f, d_out_s, dz_in, dn_in, d_f, ol_f, ol_out, ol_all, da_f, da_out, da_in,
    a_ss, a_rs, af_ss, b_ss, b_rs, t_ss, t_rs, z_ss, z_rs, n_ss, n_rs, c_ss, c_rs, ready, wt_ref,
):
    row, col = lax.axis_index("row"), lax.axis_index("col")
    chip, core = row // 2, row % 2
    partner = row + 1 - 2 * core
    tok = ti * tj
    half = ti * ti
    chips = n_row // 2
    hid = a_out.shape[-1]

    operands = (
        (pair_hbm, pair_ref), (wp_hbm, wp_ref), (gin_hbm, gin_ref), (bin_hbm, bin_ref),
        (bp_hbm, bp_ref), (mask_hbm, mask_ref), (wg_hbm, wg_ref), (bg_hbm, bg_ref),
        (cot_hbm, cot_ref), (wo_hbm, wo_ref), (gmid_hbm, gmid_ref), (bmid_hbm, bmid_ref),
        (bo_hbm, bo_ref),
    )
    loads = [
        pltpu.make_async_copy(src, dst, in_sem.at[n]) for n, (src, dst) in enumerate(operands)
    ]
    loads[0].start()
    barrier = pltpu.get_barrier_semaphore()

    def announce(to_row, to_col):
        pl.semaphore_signal(barrier, inc=1, device_id=(to_row, to_col), device_id_type=MESH)

    for step in reversed(range(1, chips)):
        announce(2 * flip(chip, step, chips) + core, col)
    announce(partner, col)
    for block in reversed(range(1, n_col)):
        @pl.when(block > col)
        def _():
            announce(row, block)

    for load in loads[1:]:
        load.start()

    def remote(src, dst, send, recv, to_row, to_col):
        return pltpu.make_async_remote_copy(
            src, dst, send, recv, device_id=(to_row, to_col), device_id_type=MESH
        )

    def reorder(ref):
        stage[...] = ref[...].astype(F32).reshape(tok, hid)
        return jnp.concatenate([stage[pl.ds(k, ti, stride=tj), :] for k in range(tj)], 0)

    loads[0].wait()
    hat_in, rstd_in = normalize(reorder(pair_ref))
    for load in loads[1:6]:
        load.wait()
    x_bf = (hat_in * gin_ref[...] + bin_ref[...]).astype(BF16)
    proj_b = dot(x_bf, wp_ref[:, 2 * hid :]) + bp_ref[:, 2 * hid :]
    mask_v = mask_ref[...].astype(F32)
    mask = jnp.concatenate(
        [jnp.broadcast_to(mask_v[:, k : k + 1], (ti, hid)) for k in range(tj)], 0
    )
    sig_b = jax.nn.sigmoid(proj_b[:, :hid])
    val_b = proj_b[:, hid:]
    b_bf = (mask * sig_b * val_b).astype(BF16)
    b_out[...] = b_bf

    pl.semaphore_wait(barrier, chips + col)

    def send_b(to):
        return remote(b_out, b_in.at[chip], b_ss.at[to], b_rs.at[chip], 2 * to + core, col)

    for step in range(chips - 1):
        send_b(jnp.where(step >= chip, step + 1, step)).start()

    for block in range(n_col - 1):
        @pl.when(block < col)
        def _():
            pl.semaphore_signal(ready, inc=1, device_id=(row, block), device_id_type=MESH)

    proj_a = dot(x_bf, wp_ref[:, : 2 * hid]) + bp_ref[:, : 2 * hid]
    sig_a = jax.nn.sigmoid(proj_a[:, :hid])
    val_a = proj_a[:, hid:]
    a_bf = (mask * sig_a * val_a).astype(BF16)
    a_out[...] = a_bf

    def send_a(step):
        to = 2 * flip(chip, step, chips) + core if step else partner
        return remote(a_out, a_in.at[chip, core], a_ss.at[step], a_rs.at[chip, core], to, col)

    def relay_a(step):
        source_chip = source(chip, step, chips)
        held = a_in.at[source_chip, core]
        return remote(held, held, af_ss.at[source_chip], a_rs.at[source_chip, core], partner, col)

    def got_a(source_chip, source_core):
        return remote(
            a_out, a_in.at[source_chip, source_core], a_ss.at[0],
            a_rs.at[source_chip, source_core], partner, col,
        )

    for step in range(chips):
        send_a(step).start()
    a_f[chip, :, core] = a_bf.astype(F32).reshape(tj, ti, hid)
    b_f[chip] = b_bf.astype(F32)

    for load in loads[6:]:
        load.wait()
    gate = jax.nn.sigmoid(dot(x_bf, wg_ref[...]) + bg_ref[...])
    grad_out = reorder(cot_ref)
    go_out[...] = (grad_out * gate).astype(BF16).reshape(2, half, hid)
    send_go = remote(go_out.at[1 - core], go_in, c_ss.at[0], c_rs.at[0], partner, col)
    send_go.start()
    dm_f[:, core] = dot_t(go_out[core], wo_ref[...]).reshape(ti, ti, hid)

    def send_tri(block):
        return remote(
            tri_out.at[block], tri_in.at[col], t_ss.at[block], t_rs.at[col], row, block
        )

    def forward(block):
        sums = []
        a_k = [[a_f[chip, k, part] for part in range(2)] for k in range(tj)]
        for jj in range(ti):
            total = [None, None]
            for k in range(tj):
                b_row = b_f[block, k * ti + jj : k * ti + jj + 1, :]
                for part in range(2):
                    term = a_k[k][part] * b_row
                    total[part] = term if k == 0 else total[part] + term
            sums += total
        whole = jnp.concatenate(sums, 0)

        @pl.when(block == col)
        def _():
            tri_own[...] = whole

        @pl.when(block != col)
        def _():
            tri_out[block] = whole.astype(BF16)
            send_tri(block).start()

    @pl.when(col < n_col - 1)
    def _():
        pl.semaphore_wait(ready, n_col - 1 - col)

    got_a(chip, 1 - core).wait_recv()
    a_f[chip, :, 1 - core] = a_in[chip, 1 - core].astype(F32).reshape(tj, ti, hid)
    forward(chip)

    def forward_step(step, carry):
        block = jnp.where(step <= chip, step - 1, step)
        remote(
            b_out, b_in.at[block], b_ss.at[0], b_rs.at[block], 2 * block + core, col
        ).wait_recv()
        b_f[block] = b_in[block].astype(F32)
        forward(block)
        return carry

    lax.fori_loop(1, chips, forward_step, 0)

    send_go.wait_recv()
    dm_f[:, 1 - core] = dot_t(go_in[...], wo_ref[...]).reshape(ti, ti, hid)
    scaled = dm_f[...].reshape(tok, hid) * gmid_ref[...]
    scaled = scaled - jnp.mean(scaled, -1, keepdims=True)

    for step in range(1, chips):
        source_chip = source(chip, step, chips)
        got_a(source_chip, core).wait_recv()
        relay_a(step).start()
        a_f[source_chip, :, core] = a_in[source_chip, core].astype(F32).reshape(tj, ti, hid)

    triangle = tri_own[...]
    for step in range(1, n_col):
        other = source(col, step, n_col)
        remote(
            tri_out.at[0], tri_in.at[other], t_ss.at[0], t_rs.at[other], row, other
        ).wait_recv()
        triangle = triangle + tri_in[other].astype(F32)
    centred = triangle - jnp.mean(triangle, -1, keepdims=True)
    variance = jnp.mean(centred * centred, -1, keepdims=True)
    slope = jnp.mean(scaled * centred, -1, keepdims=True)
    rstd_mid = lax.rsqrt(variance + 1e-05)
    hat_mid = centred * rstd_mid
    d_tri = (rstd_mid * (scaled - hat_mid * (rstd_mid * slope))).astype(BF16)
    d_out_s[...] = d_tri

    dz_in[col] = d_tri

    def send_z(block):
        return remote(d_out_s, dz_in.at[col], z_ss.at[block], z_rs.at[col], row, block)

    def send_n(block):
        return remote(
            d_out_s, dn_in.at[chip], n_ss.at[block], n_rs.at[chip], 2 * col + core, block
        )

    others = [jnp.where(step >= col, step + 1, step) for step in range(n_col - 1)]

    @pl.when(chip != col)
    def _():
        for block in others:
            send_z(block).start()
            send_n(block).start()
        send_n(col).start()

    @pl.when(chip == col)
    def _():
        for block in others:
            send_z(block).start()

    mid_bf = (hat_mid * gmid_ref[...] + bmid_ref[...]).astype(BF16)
    ol_f[...] = (dot(mid_bf, wo_ref[...]) + bo_ref[...]).reshape(ti, 2, ti, hid)
    ol_out[...] = ol_f[:, 1 - core].reshape(half, hid)
    send_ol = remote(ol_out, ol_all.at[core], c_ss.at[1], c_rs.at[1], partner, col)
    send_ol.start()
    ol_all[core] = ol_f[:, core].reshape(half, hid)

    def backward_a(block, d_block, sums):
        out = list(sums)
        for jj in range(ti):
            d_j = [d_block[(2 * jj + part) * ti : (2 * jj + part + 1) * ti] for part in range(2)]
            for k in range(tj):
                b_row = b_f[block, k * ti + jj : k * ti + jj + 1, :]
                for part in range(2):
                    out[2 * k + part] = out[2 * k + part] + d_j[part] * b_row
        return tuple(out)

    zero = tuple(jnp.zeros((ti, hid), F32) for _ in range(2 * tj))
    sums_a = backward_a(col, d_tri.astype(F32), zero)

    for step in range(1, chips):
        source_chip = source(chip, step, chips)
        got_a(source_chip, 1 - core).wait_recv()
        a_f[source_chip, :, 1 - core] = a_in[source_chip, 1 - core].astype(F32).reshape(tj, ti, hid)

    send_ol.wait_recv()
    out_lin = ol_all[...].reshape(tok, hid)
    update = gate * out_lin
    for k in range(tj):
        stage[pl.ds(k, ti, stride=tj), :] = update[k * ti : (k + 1) * ti, :]
    upd_ref[...] = stage[...].astype(BF16).reshape(ti, tj, hid)
    d_gpre = (grad_out * out_lin * gate * (1.0 - gate)).astype(BF16)
    d_x = dot_t(d_gpre, wg_ref[...])
    slope_a, gate_a = mask * val_a * sig_a * (1.0 - sig_a), mask * sig_a
    slope_b, gate_b = mask * val_b * sig_b * (1.0 - sig_b), mask * sig_b

    for part in range(2):
        wt_ref[part] = wp_ref[:, 2 * part * hid : 2 * (part + 1) * hid].T

    send_go.wait_send()
    for step in range(chips):
        send_a(step).wait_send()
    for step in range(1, chips):
        send_b(flip(chip, step, chips)).wait_send()
        relay_a(step).wait_send()
    for block in range(n_col):
        @pl.when(block != col)
        def _():
            send_tri(block).wait_send()

    def backward_step(step, sums):
        other = source(col, step, n_col)
        remote(
            d_out_s, dz_in.at[other], z_ss.at[0], z_rs.at[other], row, other
        ).wait_recv()
        return backward_a(other, dz_in[other].astype(F32), sums)

    sums_a = lax.fori_loop(1, n_col, backward_step, sums_a)
    da_f[...] = jnp.concatenate(sums_a, 0).reshape(tj, 2, ti, hid)
    da_out[...] = da_f[:, 1 - core].reshape(tok, hid)
    send_da = remote(da_out, da_in, c_ss.at[2], c_rs.at[2], partner, col)
    send_da.start()

    def backward_b(block, d_block, sums):
        d_f[...] = d_block.astype(F32)
        out = list(sums)
        for part in range(2):
            for i in range(ti):
                d_i = d_f[pl.ds(part * ti + i, ti, stride=2 * ti), :]
                for k in range(tj):
                    out[k] = out[k] + d_i * a_f[block, k, part, i : i + 1, :]
        return tuple(out)

    def backward_b_step(step, sums):
        block = source(chip, step, chips)
        remote(
            d_out_s, dn_in.at[block], n_ss.at[0], n_rs.at[block], 2 * block + core, chip
        ).wait_recv()
        return backward_b(block, dn_in[block], sums)

    zero = tuple(jnp.zeros((ti, hid), F32) for _ in range(tj))
    sums_b = backward_b(chip, dz_in[chip], zero)
    sums_b = lax.fori_loop(1, chips - 1, backward_b_step, sums_b)

    send_da.wait_recv()
    grad_a = da_f[:, core].reshape(tok, hid) + da_in[...]
    d_ga = (grad_a * slope_a).astype(BF16)
    d_va = (grad_a * gate_a).astype(BF16)
    d_x = d_x + dot(jnp.concatenate([d_ga, d_va], 1), wt_ref[0])

    sums_b = backward_b_step(chips - 1, sums_b)
    grad_b = jnp.concatenate(sums_b, 0)

    d_gb = (grad_b * slope_b).astype(BF16)
    d_vb = (grad_b * gate_b).astype(BF16)
    d_x = d_x + dot(jnp.concatenate([d_gb, d_vb], 1), wt_ref[1])
    pair_grad = norm_back(d_x, hat_in, rstd_in, gin_ref[...])
    for k in range(tj):
        grad_ref[pl.ds(k, ti, stride=tj), :] = pair_grad[k * ti : (k + 1) * ti, :]

    send_ol.wait_send()
    send_da.wait_send()
    for block in others:
        send_z(block).wait_send()

    @pl.when(chip != col)
    def _():
        for block in range(n_col):
            send_n(block).wait_send()


def store(upd_ref, grad_ref, upd_hbm, grad_hbm, sem):
    first = pltpu.make_async_copy(upd_ref, upd_hbm, sem.at[0])
    second = pltpu.make_async_copy(grad_ref, grad_hbm, sem.at[1])
    second.start()
    first.start()
    second.wait()
    first.wait()


def per_device(n_row, n_col, pair, pair_mask, gin, bin_, wp, bp, wg, bg, gmid, bmid, wo, bo, cot):
    ti, tj, chan = pair.shape
    hid = chan
    tok, half, chips = ti * tj, ti * ti, n_row // 2
    assert tj == 2 * ti and n_row == 2 * n_col
    vec = lambda v: v.reshape(1, -1)
    dma = pltpu.SemaphoreType.DMA
    vmem = pl.BlockSpec(memory_space=pltpu.VMEM)
    operands = (pair, pair_mask, vec(gin), vec(bin_), wp, vec(bp), wg, vec(bg), vec(gmid), vec(bmid), wo, vec(bo), cot)
    update, grad = pl.pallas_call(
        functools.partial(kernel, n_row, n_col, ti, tj),
        name="triangle_step",
        out_shape=(
            jax.ShapeDtypeStruct(pair.shape, BF16),
            jax.ShapeDtypeStruct((tok, hid), F32),
        ),
        in_specs=[pl.BlockSpec(memory_space=pltpu.HBM)] * 13,
        out_specs=(vmem, vmem),
        scratch_shapes=[pltpu.VMEM(v.shape, v.dtype) for v in operands]
        + [dma((len(operands),))]
        + [
            pltpu.VMEM((tok, hid), F32),
            pltpu.VMEM((tok, hid), BF16),
            pltpu.VMEM((chips, 2, tok, hid), BF16),
            pltpu.VMEM((chips, tj, 2, ti, hid), F32),
            pltpu.VMEM((tok, hid), BF16),
            pltpu.VMEM((chips, tok, hid), BF16),
            pltpu.VMEM((chips, tok, hid), F32),
            pltpu.VMEM((tok, hid), F32),
            pltpu.VMEM((n_col, tok, hid), BF16),
            pltpu.VMEM((n_col, tok, hid), BF16),
            pltpu.VMEM((2, half, hid), BF16),
            pltpu.VMEM((half, hid), BF16),
            pltpu.VMEM((ti, 2, ti, hid), F32),
            pltpu.VMEM((tok, hid), BF16),
            pltpu.VMEM((n_col, tok, hid), BF16),
            pltpu.VMEM((chips, tok, hid), BF16),
            pltpu.VMEM((tok, hid), F32),
            pltpu.VMEM((ti, 2, ti, hid), F32),
            pltpu.VMEM((half, hid), F32),
            pltpu.VMEM((2, half, hid), F32),
            pltpu.VMEM((tj, 2, ti, hid), F32),
            pltpu.VMEM((tok, hid), F32),
            pltpu.VMEM((tok, hid), F32),
            dma((chips,)),
            dma((chips, 2)),
            dma((chips,)),
            dma((chips,)),
            dma((chips,)),
            dma((n_col,)),
            dma((n_col,)),
            dma((n_col,)),
            dma((n_col,)),
            dma((n_col,)),
            dma((chips,)),
            dma((3,)),
            dma((3,)),
            pltpu.SemaphoreType.REGULAR,
            pltpu.VMEM((2, 2 * hid, chan), BF16),
        ],
        compiler_params=pltpu.CompilerParams(
            collective_id=0, has_side_effects=True, vmem_limit_bytes=40 << 20
        ),
    )(*[pltpu.with_memory_space_constraint(v, pltpu.HBM) for v in operands])
    hbm = pl.BlockSpec(memory_space=pltpu.HBM)
    update, grad = pl.pallas_call(
        store,
        name="store_outputs",
        out_shape=(
            jax.ShapeDtypeStruct(pair.shape, BF16),
            jax.ShapeDtypeStruct((tok, hid), F32),
        ),
        in_specs=[vmem, vmem],
        out_specs=(hbm, hbm),
        scratch_shapes=[dma((2,))],
        compiler_params=pltpu.CompilerParams(vmem_limit_bytes=1 << 20),
    )(update, grad)
    return update, grad.reshape(ti, tj, hid)


def solution(mesh):
    grid = P("row", "col", None)
    placed = (grid, P("row", "col")) + (P(),) * 10 + (grid,)
    return jax.shard_map(
        functools.partial(per_device, mesh.shape["row"], mesh.shape["col"]),
        mesh=mesh,
        in_specs=placed,
        out_specs=(grid, grid),
        check_vma=False,
    )
```

```python
import functools

import jax
import jax.numpy as jnp
from jax import lax
from jax.experimental import pallas as pl
from jax.experimental.pallas import tpu as pltpu
from jax.sharding import PartitionSpec as P

F32 = jnp.float32
BF16 = jnp.bfloat16
MESH = pl.DeviceIdType.MESH


def flip(index, step, size):
    if size & (size - 1):
        return lax.rem(index + step, size)
    partner, weight = 0, 1
    while weight < size:
        mine, other = (index // weight) % 2, (step // weight) % 2
        partner = partner + weight * ((mine + other) % 2)
        weight *= 2
    return partner


def source(index, step, size):
    if size & (size - 1):
        return lax.rem(index + size - step, size)
    return flip(index, step, size)


def normalize(values):
    centred = values - jnp.mean(values, -1, keepdims=True)
    inv_std = lax.rsqrt(jnp.mean(centred * centred, -1, keepdims=True) + 1e-05)
    return centred * inv_std, inv_std


def norm_back(upstream, hat, inv_std, gain):
    scaled = upstream * gain
    return inv_std * (
        scaled
        - jnp.mean(scaled, -1, keepdims=True)
        - hat * jnp.mean(scaled * hat, -1, keepdims=True)
    )


def dot(lhs, rhs):
    return jnp.dot(lhs, rhs, preferred_element_type=F32)


def dot_t(lhs, rhs):
    return lax.dot_general(lhs, rhs, (((1,), (1,)), ((), ())), preferred_element_type=F32)


def kernel(
    n_row, n_col, ti, tj,
    pair_hbm, mask_hbm, gin_hbm, bin_hbm, wp_hbm, bp_hbm, wg_hbm, bg_hbm,
    gmid_hbm, bmid_hbm, wo_hbm, bo_hbm, cot_hbm,
    upd_ref, grad_ref,
    pair_ref, mask_ref, gin_ref, bin_ref, wp_ref, bp_ref, wg_ref, bg_ref,
    gmid_ref, bmid_ref, wo_ref, bo_ref, cot_ref, in_sem,
    stage, a_out, a_in, a_f, b_out, b_in, b_f, tri_own, tri_out, tri_in,
    go_out, go_in, dm_f, d_out_s, dz_in, dn_in, d_f, ol_f, ol_out, ol_all, da_f, da_out, da_in,
    a_ss, a_rs, af_ss, b_ss, b_rs, t_ss, t_rs, z_ss, z_rs, n_ss, n_rs, c_ss, c_rs, ready, wt_ref,
):
    row, col = lax.axis_index("row"), lax.axis_index("col")
    chip, core = row // 2, row % 2
    partner = row + 1 - 2 * core
    tok = ti * tj
    half = ti * ti
    chips = n_row // 2
    hid = a_out.shape[-1]

    operands = (
        (pair_hbm, pair_ref), (wp_hbm, wp_ref), (gin_hbm, gin_ref), (bin_hbm, bin_ref),
        (bp_hbm, bp_ref), (mask_hbm, mask_ref), (wg_hbm, wg_ref), (bg_hbm, bg_ref),
        (cot_hbm, cot_ref), (wo_hbm, wo_ref), (gmid_hbm, gmid_ref), (bmid_hbm, bmid_ref),
        (bo_hbm, bo_ref),
    )
    loads = [
        pltpu.make_async_copy(src, dst, in_sem.at[n]) for n, (src, dst) in enumerate(operands)
    ]
    loads[0].start()
    barrier = pltpu.get_barrier_semaphore()

    def announce(to_row, to_col):
        pl.semaphore_signal(barrier, inc=1, device_id=(to_row, to_col), device_id_type=MESH)

    for step in reversed(range(1, chips)):
        announce(2 * flip(chip, step, chips) + core, col)
    announce(partner, col)
    for block in reversed(range(1, n_col)):
        @pl.when(block > col)
        def _():
            announce(row, block)

    for load in loads[1:]:
        load.start()

    def remote(src, dst, send, recv, to_row, to_col):
        return pltpu.make_async_remote_copy(
            src, dst, send, recv, device_id=(to_row, to_col), device_id_type=MESH
        )

    def reorder(ref):
        stage[...] = ref[...].astype(F32).reshape(tok, hid)
        return jnp.concatenate([stage[pl.ds(k, ti, stride=tj), :] for k in range(tj)], 0)

    loads[0].wait()
    hat_in, rstd_in = normalize(reorder(pair_ref))
    for load in loads[1:6]:
        load.wait()
    x_bf = (hat_in * gin_ref[...] + bin_ref[...]).astype(BF16)
    proj_b = dot(x_bf, wp_ref[:, 2 * hid :]) + bp_ref[:, 2 * hid :]
    mask_v = mask_ref[...].astype(F32)
    mask = jnp.concatenate(
        [jnp.broadcast_to(mask_v[:, k : k + 1], (ti, hid)) for k in range(tj)], 0
    )
    sig_b = jax.nn.sigmoid(proj_b[:, :hid])
    val_b = proj_b[:, hid:]
    b_bf = (mask * sig_b * val_b).astype(BF16)
    b_out[...] = b_bf

    pl.semaphore_wait(barrier, chips + col)

    def send_b(to):
        return remote(b_out, b_in.at[chip], b_ss.at[to], b_rs.at[chip], 2 * to + core, col)

    for step in range(chips - 1):
        send_b(jnp.where(step >= chip, step + 1, step)).start()

    for block in range(n_col - 1):
        @pl.when(block < col)
        def _():
            pl.semaphore_signal(ready, inc=1, device_id=(row, block), device_id_type=MESH)

    proj_a = dot(x_bf, wp_ref[:, : 2 * hid]) + bp_ref[:, : 2 * hid]
    sig_a = jax.nn.sigmoid(proj_a[:, :hid])
    val_a = proj_a[:, hid:]
    a_bf = (mask * sig_a * val_a).astype(BF16)
    a_out[...] = a_bf

    def send_a(step):
        to = 2 * flip(chip, step, chips) + core if step else partner
        return remote(a_out, a_in.at[chip, core], a_ss.at[step], a_rs.at[chip, core], to, col)

    def relay_a(step):
        source_chip = source(chip, step, chips)
        held = a_in.at[source_chip, core]
        return remote(held, held, af_ss.at[source_chip], a_rs.at[source_chip, core], partner, col)

    def got_a(source_chip, source_core):
        return remote(
            a_out, a_in.at[source_chip, source_core], a_ss.at[0],
            a_rs.at[source_chip, source_core], partner, col,
        )

    send_a(0).start()
    a_f[chip, :, core] = a_bf.astype(F32).reshape(tj, ti, hid)
    b_f[chip] = b_bf.astype(F32)

    for load in loads[6:]:
        load.wait()
    gate = jax.nn.sigmoid(dot(x_bf, wg_ref[...]) + bg_ref[...])
    grad_out = reorder(cot_ref)
    go_out[...] = (grad_out * gate).astype(BF16).reshape(2, half, hid)
    send_go = remote(go_out.at[1 - core], go_in, c_ss.at[0], c_rs.at[0], partner, col)
    send_go.start()
    dm_f[:, core] = dot_t(go_out[core], wo_ref[...]).reshape(ti, ti, hid)

    def send_tri(block):
        return remote(
            tri_out.at[block], tri_in.at[col], t_ss.at[block], t_rs.at[col], row, block
        )

    def forward(block):
        sums = []
        a_k = [[a_f[chip, k, part] for part in range(2)] for k in range(tj)]
        for jj in range(ti):
            total = [None, None]
            for k in range(tj):
                b_row = b_f[block, k * ti + jj : k * ti + jj + 1, :]
                for part in range(2):
                    term = a_k[k][part] * b_row
                    total[part] = term if k == 0 else total[part] + term
            sums += total
        whole = jnp.concatenate(sums, 0)

        @pl.when(block == col)
        def _():
            tri_own[...] = whole

        @pl.when(block != col)
        def _():
            tri_out[block] = whole.astype(BF16)
            send_tri(block).start()

    @pl.when(col < n_col - 1)
    def _():
        pl.semaphore_wait(ready, n_col - 1 - col)

    got_a(chip, 1 - core).wait_recv()
    a_f[chip, :, 1 - core] = a_in[chip, 1 - core].astype(F32).reshape(tj, ti, hid)
    forward(chip)
    for step in range(1, chips):
        send_a(step).start()

    def forward_step(step, carry):
        block = jnp.where(step <= chip, step - 1, step)
        remote(
            b_out, b_in.at[block], b_ss.at[0], b_rs.at[block], 2 * block + core, col
        ).wait_recv()
        b_f[block] = b_in[block].astype(F32)
        forward(block)
        return carry

    lax.fori_loop(1, chips, forward_step, 0)

    send_go.wait_recv()
    dm_f[:, 1 - core] = dot_t(go_in[...], wo_ref[...]).reshape(ti, ti, hid)
    scaled = dm_f[...].reshape(tok, hid) * gmid_ref[...]
    scaled = scaled - jnp.mean(scaled, -1, keepdims=True)

    for step in range(1, chips):
        source_chip = source(chip, step, chips)
        got_a(source_chip, core).wait_recv()
        relay_a(step).start()
        a_f[source_chip, :, core] = a_in[source_chip, core].astype(F32).reshape(tj, ti, hid)

    triangle = tri_own[...]
    for step in range(1, n_col):
        other = source(col, step, n_col)
        remote(
            tri_out.at[0], tri_in.at[other], t_ss.at[0], t_rs.at[other], row, other
        ).wait_recv()
        triangle = triangle + tri_in[other].astype(F32)
    centred = triangle - jnp.mean(triangle, -1, keepdims=True)
    variance = jnp.mean(centred * centred, -1, keepdims=True)
    slope = jnp.mean(scaled * centred, -1, keepdims=True)
    rstd_mid = lax.rsqrt(variance + 1e-05)
    hat_mid = centred * rstd_mid
    d_tri = (rstd_mid * (scaled - hat_mid * (rstd_mid * slope))).astype(BF16)
    d_out_s[...] = d_tri

    dz_in[col] = d_tri

    def send_z(block):
        return remote(d_out_s, dz_in.at[col], z_ss.at[block], z_rs.at[col], row, block)

    def send_n(block):
        return remote(
            d_out_s, dn_in.at[chip], n_ss.at[block], n_rs.at[chip], 2 * col + core, block
        )

    others = [jnp.where(step >= col, step + 1, step) for step in range(n_col - 1)]

    @pl.when(chip != col)
    def _():
        for block in others:
            send_z(block).start()
            send_n(block).start()
        send_n(col).start()

    @pl.when(chip == col)
    def _():
        for block in others:
            send_z(block).start()

    mid_bf = (hat_mid * gmid_ref[...] + bmid_ref[...]).astype(BF16)
    ol_f[...] = (dot(mid_bf, wo_ref[...]) + bo_ref[...]).reshape(ti, 2, ti, hid)
    ol_out[...] = ol_f[:, 1 - core].reshape(half, hid)
    send_ol = remote(ol_out, ol_all.at[core], c_ss.at[1], c_rs.at[1], partner, col)
    send_ol.start()
    ol_all[core] = ol_f[:, core].reshape(half, hid)

    def backward_a(block, d_block, sums):
        out = list(sums)
        for jj in range(ti):
            d_j = [d_block[(2 * jj + part) * ti : (2 * jj + part + 1) * ti] for part in range(2)]
            for k in range(tj):
                b_row = b_f[block, k * ti + jj : k * ti + jj + 1, :]
                for part in range(2):
                    out[2 * k + part] = out[2 * k + part] + d_j[part] * b_row
        return tuple(out)

    zero = tuple(jnp.zeros((ti, hid), F32) for _ in range(2 * tj))
    sums_a = backward_a(col, d_tri.astype(F32), zero)

    for step in range(1, chips):
        source_chip = source(chip, step, chips)
        got_a(source_chip, 1 - core).wait_recv()
        a_f[source_chip, :, 1 - core] = a_in[source_chip, 1 - core].astype(F32).reshape(tj, ti, hid)

    send_ol.wait_recv()
    out_lin = ol_all[...].reshape(tok, hid)
    update = gate * out_lin
    for k in range(tj):
        stage[pl.ds(k, ti, stride=tj), :] = update[k * ti : (k + 1) * ti, :]
    upd_ref[...] = stage[...].astype(BF16).reshape(ti, tj, hid)
    d_gpre = (grad_out * out_lin * gate * (1.0 - gate)).astype(BF16)
    d_x = dot_t(d_gpre, wg_ref[...])
    slope_a, gate_a = mask * val_a * sig_a * (1.0 - sig_a), mask * sig_a
    slope_b, gate_b = mask * val_b * sig_b * (1.0 - sig_b), mask * sig_b

    for part in range(2):
        wt_ref[part] = wp_ref[:, 2 * part * hid : 2 * (part + 1) * hid].T

    send_go.wait_send()
    for step in range(chips):
        send_a(step).wait_send()
    for step in range(1, chips):
        send_b(flip(chip, step, chips)).wait_send()
        relay_a(step).wait_send()
    for block in range(n_col):
        @pl.when(block != col)
        def _():
            send_tri(block).wait_send()

    def backward_step(step, sums):
        other = source(col, step, n_col)
        remote(
            d_out_s, dz_in.at[other], z_ss.at[0], z_rs.at[other], row, other
        ).wait_recv()
        return backward_a(other, dz_in[other].astype(F32), sums)

    sums_a = lax.fori_loop(1, n_col, backward_step, sums_a)
    da_f[...] = jnp.concatenate(sums_a, 0).reshape(tj, 2, ti, hid)
    da_out[...] = da_f[:, 1 - core].reshape(tok, hid)
    send_da = remote(da_out, da_in, c_ss.at[2], c_rs.at[2], partner, col)
    send_da.start()

    def backward_b(block, d_block, sums):
        d_f[...] = d_block.astype(F32)
        out = list(sums)
        for part in range(2):
            for i in range(ti):
                d_i = d_f[pl.ds(part * ti + i, ti, stride=2 * ti), :]
                for k in range(tj):
                    out[k] = out[k] + d_i * a_f[block, k, part, i : i + 1, :]
        return tuple(out)

    def backward_b_step(step, sums):
        block = source(chip, step, chips)
        remote(
            d_out_s, dn_in.at[block], n_ss.at[0], n_rs.at[block], 2 * block + core, chip
        ).wait_recv()
        return backward_b(block, dn_in[block], sums)

    zero = tuple(jnp.zeros((ti, hid), F32) for _ in range(tj))
    sums_b = backward_b(chip, dz_in[chip], zero)
    sums_b = lax.fori_loop(1, chips - 1, backward_b_step, sums_b)

    send_da.wait_recv()
    grad_a = da_f[:, core].reshape(tok, hid) + da_in[...]
    d_ga = (grad_a * slope_a).astype(BF16)
    d_va = (grad_a * gate_a).astype(BF16)
    d_x = d_x + dot(jnp.concatenate([d_ga, d_va], 1), wt_ref[0])

    sums_b = backward_b_step(chips - 1, sums_b)
    grad_b = jnp.concatenate(sums_b, 0)

    d_gb = (grad_b * slope_b).astype(BF16)
    d_vb = (grad_b * gate_b).astype(BF16)
    d_x = d_x + dot(jnp.concatenate([d_gb, d_vb], 1), wt_ref[1])
    pair_grad = norm_back(d_x, hat_in, rstd_in, gin_ref[...])
    for k in range(tj):
        grad_ref[pl.ds(k, ti, stride=tj), :] = pair_grad[k * ti : (k + 1) * ti, :]

    send_ol.wait_send()
    send_da.wait_send()
    for block in others:
        send_z(block).wait_send()

    @pl.when(chip != col)
    def _():
        for block in range(n_col):
            send_n(block).wait_send()


def store(upd_ref, grad_ref, upd_hbm, grad_hbm, sem):
    first = pltpu.make_async_copy(upd_ref, upd_hbm, sem.at[0])
    second = pltpu.make_async_copy(grad_ref, grad_hbm, sem.at[1])
    second.start()
    first.start()
    second.wait()
    first.wait()


def per_device(n_row, n_col, pair, pair_mask, gin, bin_, wp, bp, wg, bg, gmid, bmid, wo, bo, cot):
    ti, tj, chan = pair.shape
    hid = chan
    tok, half, chips = ti * tj, ti * ti, n_row // 2
    assert tj == 2 * ti and n_row == 2 * n_col
    vec = lambda v: v.reshape(1, -1)
    dma = pltpu.SemaphoreType.DMA
    vmem = pl.BlockSpec(memory_space=pltpu.VMEM)
    operands = (pair, pair_mask, vec(gin), vec(bin_), wp, vec(bp), wg, vec(bg), vec(gmid), vec(bmid), wo, vec(bo), cot)
    update, grad = pl.pallas_call(
        functools.partial(kernel, n_row, n_col, ti, tj),
        name="triangle_step",
        out_shape=(
            jax.ShapeDtypeStruct(pair.shape, BF16),
            jax.ShapeDtypeStruct((tok, hid), F32),
        ),
        in_specs=[pl.BlockSpec(memory_space=pltpu.HBM)] * 13,
        out_specs=(vmem, vmem),
        scratch_shapes=[pltpu.VMEM(v.shape, v.dtype) for v in operands]
        + [dma((len(operands),))]
        + [
            pltpu.VMEM((tok, hid), F32),
            pltpu.VMEM((tok, hid), BF16),
            pltpu.VMEM((chips, 2, tok, hid), BF16),
            pltpu.VMEM((chips, tj, 2, ti, hid), F32),
            pltpu.VMEM((tok, hid), BF16),
            pltpu.VMEM((chips, tok, hid), BF16),
            pltpu.VMEM((chips, tok, hid), F32),
            pltpu.VMEM((tok, hid), F32),
            pltpu.VMEM((n_col, tok, hid), BF16),
            pltpu.VMEM((n_col, tok, hid), BF16),
            pltpu.VMEM((2, half, hid), BF16),
            pltpu.VMEM((half, hid), BF16),
            pltpu.VMEM((ti, 2, ti, hid), F32),
            pltpu.VMEM((tok, hid), BF16),
            pltpu.VMEM((n_col, tok, hid), BF16),
            pltpu.VMEM((chips, tok, hid), BF16),
            pltpu.VMEM((tok, hid), F32),
            pltpu.VMEM((ti, 2, ti, hid), F32),
            pltpu.VMEM((half, hid), F32),
            pltpu.VMEM((2, half, hid), F32),
            pltpu.VMEM((tj, 2, ti, hid), F32),
            pltpu.VMEM((tok, hid), F32),
            pltpu.VMEM((tok, hid), F32),
            dma((chips,)),
            dma((chips, 2)),
            dma((chips,)),
            dma((chips,)),
            dma((chips,)),
            dma((n_col,)),
            dma((n_col,)),
            dma((n_col,)),
            dma((n_col,)),
            dma((n_col,)),
            dma((chips,)),
            dma((3,)),
            dma((3,)),
            pltpu.SemaphoreType.REGULAR,
            pltpu.VMEM((2, 2 * hid, chan), BF16),
        ],
        compiler_params=pltpu.CompilerParams(
            collective_id=0, has_side_effects=True, vmem_limit_bytes=40 << 20
        ),
    )(*[pltpu.with_memory_space_constraint(v, pltpu.HBM) for v in operands])
    hbm = pl.BlockSpec(memory_space=pltpu.HBM)
    update, grad = pl.pallas_call(
        store,
        name="store_outputs",
        out_shape=(
            jax.ShapeDtypeStruct(pair.shape, BF16),
            jax.ShapeDtypeStruct((tok, hid), F32),
        ),
        in_specs=[vmem, vmem],
        out_specs=(hbm, hbm),
        scratch_shapes=[dma((2,))],
        compiler_params=pltpu.CompilerParams(vmem_limit_bytes=1 << 20),
    )(update, grad)
    return update, grad.reshape(ti, tj, hid)


def solution(mesh):
    grid = P("row", "col", None)
    placed = (grid, P("row", "col")) + (P(),) * 10 + (grid,)
    return jax.shard_map(
        functools.partial(per_device, mesh.shape["row"], mesh.shape["col"]),
        mesh=mesh,
        in_specs=placed,
        out_specs=(grid, grid),
        check_vma=False,
    )
```
